256 devices in a mesh: tp: 8 (over x, z_hi), cp: 32 (over z_lo, y, core).
Axes of the slice: x: 4, y: 4, z: 8 (z_hi: 2, z_lo: 4; z = z_hi * 4 + z_lo), core: 2. Of those that a mesh axis runs over, the one named last changes fastest.
Arguments:
- signal: bfloat16 [4096, 4096], P('cp', 'tp'), may hold values from -6 to 6
- cotangent: bfloat16 [4096, 4096], P('cp', 'tp'), may hold values from -0.09375 to 0.09375
- long_filter: bfloat16 [4096, 512], P('cp'), may hold values from -6 to 6
Outputs:
- grad_signal: bfloat16 [4096, 4096], P('cp', 'tp')
- grad_filter: bfloat16 [4096, 512], P('cp')
The draws below stay inside these ranges and needn't reach their ends.
All inputs are finite; a program needn't handle non-finite values.
Results may differ from the reference program's by a relative error of at most 0.0015.
Values may be sent and summed in bfloat16 or wider, within the bound.
A program may use at most 64 MiB of HBM per device.

```python
import math
import jax
import jax.numpy as jnp
from jax import lax

CHANNELS = 4096
FILTERS = 512
SEQ = 4096


def shard_levels(rng, extent, shards, smallest, top_value):
    level, own = 1.0, jax.random.fold_in(rng, 6)
    for position, parts in shards:
        steps = jnp.exp(jax.random.uniform(jax.random.fold_in(own, position), (parts,), jnp.float32, smallest / len(shards), top_value / len(shards)))
        level = level * jnp.repeat(steps, extent[position] // parts).reshape([-1 if axis == position else 1 for axis in range(len(extent))])
    return level


def gaussian(key, extent, width, limit, pieces=(), dtype=jnp.bfloat16):
    loudness = shard_levels(key, extent, pieces, -0.22, 0.18) if pieces else 1.0
    array = jax.random.normal(key, extent, jnp.float32) * width * loudness
    return jnp.minimum(jnp.maximum(array, -limit), limit).astype(dtype)


def setup_inputs(seed: int = 0) -> dict:
    seeds = jax.random.split(jax.random.key(seed), 4)
    return {
        "signal": gaussian(seeds[0], (SEQ, CHANNELS), 1.0, 6.0, ((0, 32), (1, 8))),
        "cotangent": gaussian(seeds[1], (SEQ, CHANNELS), (SEQ ** -0.5), 0.09375, ((0, 32), (1, 8))),
        "long_filter": gaussian(seeds[2], (SEQ, FILTERS), 1.0, 6.0, ((0, 32),)),
    }


def filter_block(operands):
    sig_block, cot_block, fil_block = operands
    length = 2 * SEQ
    spec_sig = jnp.fft.rfft(sig_block.astype(jnp.float32), n=length, axis=0)
    spec_cot = jnp.fft.rfft(cot_block.astype(jnp.float32), n=length, axis=0)
    spec_fil = jnp.fft.rfft(fil_block.astype(jnp.float32), n=length, axis=0)
    grad_sig = jnp.fft.irfft(jnp.conj(spec_fil)[:, None, :] * spec_cot, n=length, axis=0)[:SEQ]
    summed = jnp.sum(jnp.conj(spec_sig) * spec_cot, axis=1)
    grad_fil = jnp.fft.irfft(summed, n=length, axis=0)[:SEQ]
    return grad_sig.astype(jnp.bfloat16), grad_fil.astype(jnp.bfloat16)


def reference(signal, cotangent, long_filter):
    groups = CHANNELS // FILTERS
    block_cols = math.gcd(FILTERS, 64)
    blocks = FILTERS // block_cols

    def arrange(matrix):
        return matrix.reshape(SEQ, groups, blocks, block_cols).transpose(2, 0, 1, 3)

    filters = long_filter.reshape(SEQ, blocks, block_cols).transpose(1, 0, 2)
    grad_sig, grad_fil = lax.map(filter_block, (arrange(signal), arrange(cotangent), filters))
    grad_signal = grad_sig.transpose(1, 2, 0, 3).reshape(SEQ, CHANNELS)
    grad_filter = grad_fil.transpose(1, 0, 2).reshape(SEQ, FILTERS)
    return grad_signal, grad_filter
```

```python
import functools

import jax
import jax.numpy as jnp
import ml_dtypes
import numpy as np
from jax import lax
from jax.experimental import pallas as pl
from jax.experimental.pallas import tpu as pltpu
from jax.sharding import PartitionSpec as P

MESH = pl.DeviceIdType.MESH
bf16, f32 = jnp.bfloat16, jnp.float32
LANES = 128


def split_np(table):
    high = table.astype(ml_dtypes.bfloat16)
    low = (table - high.astype(np.float64)).astype(ml_dtypes.bfloat16)
    return high, low


def make_tables(blocks):
    half = 2 * blocks
    total = half * LANES
    w = np.arange(blocks) + 0.5
    k = np.arange(blocks)
    angle = 2 * np.pi * np.outer(w, k) / half
    pair = np.eye(2)
    cos_wk, sin_wk = np.kron(np.cos(angle), pair), np.kron(np.sin(angle), pair)
    filt = np.concatenate([cos_wk, -sin_wk], axis=0)
    both = np.zeros((2, 2, blocks, 2, blocks, 2, 2))
    for a in range(2):
        for c in range(2):
            both[a, 0, :, c, :, a, c] = np.cos(angle)
            both[a, 1, :, c, :, a, c] = -np.sin(angle)
    both = both.reshape(8 * blocks, 4 * blocks)
    lane = np.arange(LANES)
    twist = 2 * np.pi * np.outer(np.repeat(w, 2), lane) / total
    turn = 2 * np.pi * np.outer(lane, lane) / LANES
    cos_t, sin_t = np.cos(turn), np.sin(turn)
    forward = np.block([[cos_t, -sin_t], [sin_t, cos_t]])
    back = np.concatenate([cos_wk.T, -sin_wk.T], axis=1) * (2.0 / total)
    both_h, both_l = split_np(both)
    filt_h, filt_l = split_np(filt)
    forw_h, forw_l = split_np(forward)
    inv_h, inv_l = split_np(forward.T)
    back_h, back_l = split_np(back)
    tables = (
        np.concatenate([both_h, both_l], axis=1),
        np.concatenate([filt_h, filt_l], axis=1),
        np.stack([np.cos(twist), np.sin(twist)]).astype(np.float32),
        np.stack([forw_h, forw_l]),
        np.stack([inv_h, inv_l]),
        np.concatenate([back_h, back_h, back_l], axis=1),
    )
    return tables


def permutation(groups):
    table = np.zeros((groups, 2, 2, 2, groups, 2), np.float32)
    for d in range(groups):
        for a in range(2):
            for c in range(2):
                table[d, a, c, a, d, c] = 1
    return table.reshape(4 * groups, 4 * groups)


def dot(left, right):
    return lax.dot_general(left, right, (((1,), (0,)), ((), ())), preferred_element_type=f32)


def dot_nt(left, right):
    return lax.dot_general(left, right, (((1,), (1,)), ((), ())), preferred_element_type=f32)


def split(value):
    high = value.astype(bf16)
    low = (value - high.astype(f32)).astype(bf16)
    return high, low


def dot3(value, table_ref):
    high, low = split(value)
    top, bottom = table_ref[0], table_ref[1]
    return dot(high, top) + (dot(low, top) + dot(high, bottom))


def exchange(
    groups,
    blocks,
    sig_hbm,
    cot_hbm,
    fil_hbm,
    *refs,
):
    tables_hbm, rest = refs[:7], refs[7:]
    out_ref = rest[0]
    sig, cot, fil = rest[1:4]
    both, filt, twist, forw, inv, back, perm = rest[4:11]
    (send, send_f, recv, recv_f, ready, back_in) = rest[11:17]
    (load_sem, send_sem, recv_sem, send_f_sem, recv_f_sem, out_sem, in_sem, exit_sem) = rest[17:]
    t = lax.axis_index("tp")
    p = lax.axis_index("cp")
    me = t * blocks + p
    devices = groups * blocks

    def peers(act):
        def group_step(a, _):
            group = lax.rem(t + a, groups)

            def place_step(b, _):
                place = lax.rem(p + b, blocks)
                act(group, place)
                return 0

            lax.fori_loop(jnp.where(a == 0, 1, 0), blocks, place_step, 0)
            return 0

        lax.fori_loop(0, groups, group_step, 0)

    loads = [
        pltpu.make_async_copy(source, target, load_sem.at[i])
        for i, (source, target) in enumerate(
            zip(
                (sig_hbm, cot_hbm, fil_hbm) + tuple(tables_hbm),
                (sig, cot, fil, both, filt, twist, forw, inv, back, perm),
                strict=True,
            )
        )
    ]
    for load in loads:
        load.start()

    barrier = pltpu.get_barrier_semaphore()

    def greet(group, place):
        pl.semaphore_signal(barrier, inc=1, device_id=(group, place), device_id_type=MESH)

    peers(greet)
    for load in loads:
        load.wait()

    rows = perm[...]
    eye = (
        lax.broadcasted_iota(jnp.int32, (LANES, LANES), 0)
        == lax.broadcasted_iota(jnp.int32, (LANES, LANES), 1)
    ).astype(f32).astype(bf16)
    quarters = 2 * devices // LANES
    per = LANES // 2
    for q in range(quarters):
        cols = pl.ds(q * LANES, LANES)
        pair = jnp.concatenate([sig[:, cols], cot[:, cols]], axis=1)
        moved = dot_nt(rows, pair)
        send[pl.ds(q * per, per)] = moved.reshape(per, 4, LANES).astype(bf16)
        moved = dot_nt(eye, fil[:, cols])
        send_f[pl.ds(q * per, per)] = moved.reshape(per, 2, LANES).astype(bf16)

    pl.semaphore_wait(barrier, devices - 1)

    pltpu.make_async_copy(send_f.at[me], recv_f.at[p], recv_f_sem).start()

    def filter_step(b, _):
        place = lax.rem(p + b, blocks)
        pltpu.make_async_remote_copy(
            send_f.at[t * blocks + place],
            recv_f.at[p],
            send_f_sem,
            recv_f_sem,
            device_id=(t, place),
            device_id_type=MESH,
        ).start()
        return 0

    lax.fori_loop(1, blocks, filter_step, 0)
    pltpu.make_async_copy(send.at[me], recv.at[me], recv_sem).start()

    def give(group, place):
        pltpu.make_async_remote_copy(
            send.at[group * blocks + place],
            recv.at[me],
            send_sem,
            recv_sem,
            device_id=(group, place),
            device_id_type=MESH,
        ).start()

    peers(give)

    turn_c, turn_s = twist[0], twist[1]
    width = 2 * blocks

    def spectrum(real, imag):
        turned = jnp.concatenate(
            [real * turn_c + imag * turn_s, imag * turn_c - real * turn_s], axis=1
        )
        return dot3(turned, forw)

    pltpu.make_async_copy(recv_f, recv_f, recv_f_sem).wait()
    data = recv_f[...].reshape(2 * blocks, LANES)
    halves = dot(filt[...], jnp.concatenate([data, data], axis=0))
    h_spec = spectrum(halves[:width], halves[width:])
    h_real, h_imag = h_spec[:, :LANES], h_spec[:, LANES:]

    pltpu.make_async_copy(recv, recv, recv_sem).wait()
    sum_real = jnp.zeros((width, LANES), f32)
    sum_imag = jnp.zeros((width, LANES), f32)

    def inverse(real, imag):
        part = dot3(jnp.concatenate([real, imag], axis=1), inv)
        g_real, g_imag = part[:, :LANES], part[:, LANES:]
        turned = jnp.concatenate(
            [g_real * turn_c - g_imag * turn_s, g_real * turn_s + g_imag * turn_c], axis=0
        )
        high, low = split(turned)
        return dot(back[...], jnp.concatenate([high, low, high], axis=0))

    results = []
    for g in range(groups):
        data = recv[pl.ds(g * blocks, blocks)].reshape(4 * blocks, LANES)
        halves = dot(both[...], jnp.concatenate([data, data], axis=0))
        u_spec = spectrum(halves[:width], halves[width : 2 * width])
        d_spec = spectrum(halves[2 * width : 3 * width], halves[3 * width :])
        u_real, u_imag = u_spec[:, :LANES], u_spec[:, LANES:]
        d_real, d_imag = d_spec[:, :LANES], d_spec[:, LANES:]
        sum_real = sum_real + (u_real * d_real + u_imag * d_imag)
        sum_imag = sum_imag + (u_real * d_imag - u_imag * d_real)
        results.append(
            inverse(h_real * d_real + h_imag * d_imag, h_real * d_imag - h_imag * d_real)
        )
    gf = inverse(sum_real, sum_imag).reshape(blocks, 2, LANES)
    for g in range(groups):
        gs = results[g].reshape(blocks, 2, LANES)
        ready[pl.ds(g * blocks, blocks)] = jnp.concatenate([gs, gf], axis=1).astype(bf16)

    pltpu.make_async_copy(ready.at[me], back_in.at[me], in_sem).start()

    def give_back(group, place):
        pltpu.make_async_remote_copy(
            ready.at[group * blocks + place],
            back_in.at[me],
            out_sem,
            in_sem,
            device_id=(group, place),
            device_id_type=MESH,
        ).start()

    peers(give_back)
    pltpu.make_async_copy(back_in, back_in, in_sem).wait()
    done = pltpu.make_async_copy(back_in, out_ref, exit_sem)
    done.start()
    some = pl.ds(0, devices - 1)
    pltpu.make_async_copy(send.at[some], send.at[some], send_sem).wait()
    pltpu.make_async_copy(ready.at[some], ready.at[some], out_sem).wait()
    some = pl.ds(0, blocks - 1)
    pltpu.make_async_copy(send_f.at[some], send_f.at[some], send_f_sem).wait()
    done.wait()


def place_columns(quarters, in_ref, perm_ref, gs_ref, gf_ref):
    eye = (
        lax.broadcasted_iota(jnp.int32, (LANES, LANES), 0)
        == lax.broadcasted_iota(jnp.int32, (LANES, LANES), 1)
    ).astype(f32).astype(bf16)
    per = LANES // 2
    for q in range(quarters):
        block = in_ref[pl.ds(q * per, per)].reshape(4 * per, LANES)
        moved = dot_nt(eye, dot(perm_ref[...], block).astype(bf16)).astype(bf16)
        gs_ref[:, pl.ds(q * LANES, LANES)] = moved[:, :LANES]
        gf_ref[:, pl.ds(q * LANES, LANES)] = moved[:, LANES:]


def body(groups, blocks, signal, cotangent, long_filter):
    positions, columns = signal.shape
    devices = groups * blocks
    tables = make_tables(blocks)
    perm = permutation(LANES // 2)
    tables = tables + (perm.astype(ml_dtypes.bfloat16),)
    vmem = pltpu.VMEM
    dma = pltpu.SemaphoreType.DMA
    anywhere = pl.BlockSpec(memory_space=pl.ANY)
    width = 2 * blocks
    moved = pl.pallas_call(
        functools.partial(exchange, groups, blocks),
        name="exchange",
        out_shape=jax.ShapeDtypeStruct((devices, 4, LANES), bf16),
        in_specs=[anywhere] * (3 + len(tables)),
        out_specs=anywhere,
        scratch_shapes=[vmem((positions, columns), bf16)] * 3
        + [vmem(table.shape, table.dtype) for table in tables]
        + [
            vmem((devices, 4, LANES), bf16),
            vmem((devices, 2, LANES), bf16),
            vmem((devices, 4, LANES), bf16),
            vmem((blocks, 2, LANES), bf16),
            vmem((devices, 4, LANES), bf16),
            vmem((devices, 4, LANES), bf16),
            dma((3 + len(tables),)),
            dma(()),
            dma(()),
            dma(()),
            dma(()),
            dma(()),
            dma(()),
            dma(()),
        ],
        compiler_params=pltpu.CompilerParams(collective_id=0, has_side_effects=True),
    )(signal, cotangent, long_filter, *[jnp.asarray(table) for table in tables])
    whole = pl.BlockSpec(memory_space=pltpu.VMEM)
    return pl.pallas_call(
        functools.partial(place_columns, columns // LANES),
        name="place_columns",
        out_shape=(
            jax.ShapeDtypeStruct((positions, columns), bf16),
            jax.ShapeDtypeStruct((positions, columns), bf16),
        ),
        in_specs=[whole] * 2,
        out_specs=(whole, whole),
    )(moved, jnp.asarray(np.ascontiguousarray(perm.T).astype(ml_dtypes.bfloat16)))


def solution(mesh):
    in_specs = (P("cp", "tp"), P("cp", "tp"), P("cp", None))
    out_specs = (P("cp", "tp"), P("cp", None))
    run = functools.partial(body, mesh.shape["tp"], mesh.shape["cp"])
    return jax.shard_map(run, mesh=mesh, in_specs=in_specs, out_specs=out_specs, check_vma=False)
```

```python
import functools

import jax
import jax.numpy as jnp
import ml_dtypes
import numpy as np
from jax import lax
from jax.experimental import pallas as pl
from jax.experimental.pallas import tpu as pltpu
from jax.sharding import PartitionSpec as P

MESH = pl.DeviceIdType.MESH
bf16, f32 = jnp.bfloat16, jnp.float32
LANES = 128


def split_np(table):
    high = table.astype(ml_dtypes.bfloat16)
    low = (table - high.astype(np.float64)).astype(ml_dtypes.bfloat16)
    return high, low


def make_tables(blocks):
    half = 2 * blocks
    total = half * LANES
    w = np.arange(blocks) + 0.5
    k = np.arange(blocks)
    angle = 2 * np.pi * np.outer(w, k) / half
    pair = np.eye(2)
    cos_wk, sin_wk = np.kron(np.cos(angle), pair), np.kron(np.sin(angle), pair)
    filt = np.concatenate([cos_wk, -sin_wk], axis=0)
    both = np.zeros((2, 2, blocks, 2, blocks, 2, 2))
    for a in range(2):
        for c in range(2):
            both[a, 0, :, c, :, a, c] = np.cos(angle)
            both[a, 1, :, c, :, a, c] = -np.sin(angle)
    both = both.reshape(8 * blocks, 4 * blocks)
    lane = np.arange(LANES)
    twist = 2 * np.pi * np.outer(np.repeat(w, 2), lane) / total
    turn = 2 * np.pi * np.outer(lane, lane) / LANES
    cos_t, sin_t = np.cos(turn), np.sin(turn)
    forward = np.block([[cos_t, -sin_t], [sin_t, cos_t]])
    back = np.concatenate([cos_wk.T, -sin_wk.T], axis=1) * (2.0 / total)
    both_h, both_l = split_np(both)
    filt_h, filt_l = split_np(filt)
    forw_h, forw_l = split_np(forward)
    inv_h, inv_l = split_np(forward.T)
    back_h, back_l = split_np(back)
    tables = (
        np.concatenate([both_h, both_l], axis=1),
        np.concatenate([filt_h, filt_l], axis=1),
        np.stack([np.cos(twist), np.sin(twist)]).astype(np.float32),
        np.stack([forw_h, forw_l]),
        np.stack([inv_h, inv_l]),
        np.concatenate([back_h, back_h, back_l], axis=1),
    )
    return tables


def permutation(groups):
    table = np.zeros((groups, 2, 2, 2, groups, 2), np.float32)
    for d in range(groups):
        for a in range(2):
            for c in range(2):
                table[d, a, c, a, d, c] = 1
    return table.reshape(4 * groups, 4 * groups)


def dot(left, right):
    return lax.dot_general(left, right, (((1,), (0,)), ((), ())), preferred_element_type=f32)


def dot_nt(left, right):
    return lax.dot_general(left, right, (((1,), (1,)), ((), ())), preferred_element_type=f32)


def split(value):
    high = value.astype(bf16)
    low = (value - high.astype(f32)).astype(bf16)
    return high, low


def dot3(value, table_ref):
    high, low = split(value)
    top, bottom = table_ref[0], table_ref[1]
    return dot(high, top) + (dot(low, top) + dot(high, bottom))


def far_first(size):
    return sorted(range(size), key=lambda o: -min(o, size - o))


def exchange(groups, blocks, sig_hbm, cot_hbm, fil_hbm, *refs):
    tables_hbm, rest = refs[:7], refs[7:]
    out_gs, out_gf = rest[:2]
    sig, cot, fil = rest[2:5]
    both, filt, twist, forw, inv, back, perm = rest[5:12]
    (send, send_f, recv, recv_f, ready, ready_f) = rest[12:18]
    (load_sem, send_sem, recv_sem, send_f_sem, recv_f_sem) = rest[18:23]
    (gs_out_sem, gs_in_sem, gf_out_sem, gf_in_sem) = rest[23:]
    t = lax.axis_index("tp")
    p = lax.axis_index("cp")
    me = t * blocks + p
    devices = groups * blocks
    xs, lows = groups // 2, blocks // 8
    x, high = t // 2, lax.rem(t, 2)
    z, rest_p = high * lows + p // 8, lax.rem(p, 8)

    def greet_all():
        barrier = pltpu.get_barrier_semaphore()
        for z_off in far_first(2 * lows):
            z_to = lax.rem(z + z_off, 2 * lows)
            for x_off in far_first(xs):
                group = lax.rem(x + x_off, xs) * 2 + z_to // lows
                base = lax.rem(z_to, lows) * 8

                def greet(i, _, group=group, base=base):
                    place = base + lax.rem(rest_p + i, 8)
                    pl.semaphore_signal(
                        barrier, inc=1, device_id=(group, place), device_id_type=MESH
                    )
                    return 0

                lax.fori_loop(1 if z_off == 0 and x_off == 0 else 0, 8, greet, 0)

    steps = [(x_off, h_off) for x_off in far_first(xs) for h_off in (1, 0)]
    steps = sorted(steps, key=lambda o: min(o[0], xs - o[0]) + 0.5 * o[1])

    def there(step):
        return lax.rem(x + step[0], xs) * 2 + lax.rem(high + step[1], 2)

    def origin(step):
        return lax.rem(x + xs - step[0], xs) * 2 + lax.rem(high + step[1], 2)

    def places(step, act):
        def one(i, _):
            act(lax.rem(p + i, blocks))
            return 0

        lax.fori_loop(1 if step == (0, 0) else 0, blocks, one, 0)

    loads = [
        pltpu.make_async_copy(source, target, load_sem.at[i])
        for i, (source, target) in enumerate(
            zip(
                (sig_hbm, cot_hbm, fil_hbm) + tuple(tables_hbm),
                (sig, cot, fil, both, filt, twist, forw, inv, back, perm),
                strict=True,
            )
        )
    ]
    for load in loads:
        load.start()
    greet_all()
    for load in loads:
        load.wait()

    eye = identity()
    per = LANES // 2
    for q in range(2 * devices // LANES):
        cols = pl.ds(q * LANES, LANES)
        pair = jnp.concatenate([sig[:, cols], cot[:, cols]], axis=1)
        moved = dot_nt(perm[...], pair)
        send[pl.ds(q * per, per)] = moved.reshape(per, 4, LANES).astype(bf16)
        moved = dot_nt(eye, fil[:, cols])
        send_f[pl.ds(q * per, per)] = moved.reshape(per, 2, LANES).astype(bf16)

    pl.semaphore_wait(pltpu.get_barrier_semaphore(), devices - 1)

    pltpu.make_async_copy(send_f.at[me], recv_f.at[p], recv_f_sem).start()

    def give_filter(place):
        pltpu.make_async_remote_copy(
            send_f.at[t * blocks + place],
            recv_f.at[p],
            send_f_sem,
            recv_f_sem,
            device_id=(t, place),
            device_id_type=MESH,
        ).start()

    places((0, 0), give_filter)
    for n, step in enumerate(steps):
        group = there(step)

        def give(place, n=n, group=group):
            pltpu.make_async_remote_copy(
                send.at[group * blocks + place],
                recv.at[me],
                send_sem,
                recv_sem.at[n],
                device_id=(group, place),
                device_id_type=MESH,
            ).start()

        places(step, give)
        if step == (0, 0):
            pltpu.make_async_copy(send.at[me], recv.at[me], recv_sem.at[n]).start()

    turn_c, turn_s = twist[0], twist[1]
    width = 2 * blocks

    def spectrum(real, imag):
        turned = jnp.concatenate(
            [real * turn_c + imag * turn_s, imag * turn_c - real * turn_s], axis=1
        )
        return dot3(turned, forw)

    def inverse(real, imag):
        part = dot3(jnp.concatenate([real, imag], axis=1), inv)
        g_real, g_imag = part[:, :LANES], part[:, LANES:]
        turned = jnp.concatenate(
            [g_real * turn_c - g_imag * turn_s, g_real * turn_s + g_imag * turn_c], axis=0
        )
        high_part, low_part = split(turned)
        result = dot(back[...], jnp.concatenate([high_part, low_part, high_part], axis=0))
        return result.reshape(blocks, 2, LANES).astype(bf16)

    pltpu.make_async_copy(recv_f, recv_f, recv_f_sem).wait()
    data = recv_f[...].reshape(2 * blocks, LANES)
    halves = dot(filt[...], jnp.concatenate([data, data], axis=0))
    h_spec = spectrum(halves[:width], halves[width:])
    h_real, h_imag = h_spec[:, :LANES], h_spec[:, LANES:]

    sum_real = jnp.zeros((width, LANES), f32)
    sum_imag = jnp.zeros((width, LANES), f32)
    for n, step in enumerate(steps):
        group = origin(step)
        mine = pl.ds(group * blocks, blocks)
        pltpu.make_async_copy(recv.at[mine], recv.at[mine], recv_sem.at[n]).wait()
        data = recv[mine].reshape(4 * blocks, LANES)
        halves = dot(both[...], jnp.concatenate([data, data], axis=0))
        real = jnp.concatenate([halves[:width], halves[2 * width : 3 * width]], axis=0)
        imag = jnp.concatenate([halves[width : 2 * width], halves[3 * width :]], axis=0)
        cos2 = jnp.concatenate([turn_c, turn_c], axis=0)
        sin2 = jnp.concatenate([turn_s, turn_s], axis=0)
        turned = jnp.concatenate(
            [real * cos2 + imag * sin2, imag * cos2 - real * sin2], axis=1
        )
        spec = dot3(turned, forw)
        u_real, u_imag = spec[:width, :LANES], spec[:width, LANES:]
        d_real, d_imag = spec[width:, :LANES], spec[width:, LANES:]
        sum_real = sum_real + (u_real * d_real + u_imag * d_imag)
        sum_imag = sum_imag + (u_real * d_imag - u_imag * d_real)
        if n == len(steps) - 1:
            ready_f[...] = inverse(sum_real, sum_imag)
            for last in steps[::-1]:
                target = origin(last)

                def give_last(place, target=target):
                    pltpu.make_async_remote_copy(
                        ready_f.at[place],
                        out_gf.at[me],
                        gf_out_sem,
                        gf_in_sem,
                        device_id=(target, place),
                        device_id_type=MESH,
                    ).start()

                places(last, give_last)
            pltpu.make_async_copy(ready_f.at[p], out_gf.at[me], gf_in_sem).start()
        ready[mine] = inverse(
            h_real * d_real + h_imag * d_imag, h_real * d_imag - h_imag * d_real
        )

        def give_back(place, group=group):
            pltpu.make_async_remote_copy(
                ready.at[group * blocks + place],
                out_gs.at[me],
                gs_out_sem,
                gs_in_sem,
                device_id=(group, place),
                device_id_type=MESH,
            ).start()

        places(step, give_back)
        if step == (0, 0):
            pltpu.make_async_copy(ready.at[me], out_gs.at[me], gs_in_sem).start()

    some = pl.ds(0, devices - 1)
    pltpu.make_async_copy(send.at[some], send.at[some], send_sem).wait()
    pltpu.make_async_copy(ready.at[some], ready.at[some], gs_out_sem).wait()
    few = pl.ds(0, blocks - 1)
    pltpu.make_async_copy(send_f.at[few], send_f.at[few], send_f_sem).wait()
    pltpu.make_async_copy(out_gf.at[some], out_gf.at[some], gf_out_sem).wait()
    pltpu.make_async_copy(out_gs, out_gs, gs_in_sem).wait()
    pltpu.make_async_copy(out_gf, out_gf, gf_in_sem).wait()


def identity():
    rows = lax.broadcasted_iota(jnp.int32, (LANES, LANES), 0)
    cols = lax.broadcasted_iota(jnp.int32, (LANES, LANES), 1)
    return (rows == cols).astype(f32).astype(bf16)


def place_columns(quarters, gs_in, gf_in, gs_ref, gf_ref):
    eye = identity()
    per = LANES // 2
    for q in range(quarters):
        for source, target in ((gs_in, gs_ref), (gf_in, gf_ref)):
            block = source[pl.ds(q * per, per)].reshape(LANES, LANES)
            target[:, pl.ds(q * LANES, LANES)] = dot_nt(eye, block).astype(bf16)


def body(groups, blocks, signal, cotangent, long_filter):
    positions, columns = signal.shape
    devices = groups * blocks
    tables = make_tables(blocks) + (permutation(LANES // 2).astype(ml_dtypes.bfloat16),)
    vmem = pltpu.VMEM
    dma = pltpu.SemaphoreType.DMA
    anywhere = pl.BlockSpec(memory_space=pl.ANY)
    whole = pl.BlockSpec(memory_space=pltpu.VMEM)
    pairs = pltpu.VMEM((devices, 2, LANES), bf16)
    gs_rows, gf_rows = pl.pallas_call(
        functools.partial(exchange, groups, blocks),
        name="exchange",
        out_shape=(pairs, pairs),
        in_specs=[anywhere] * (3 + len(tables)),
        out_specs=(whole, whole),
        scratch_shapes=[vmem((positions, columns), bf16)] * 3
        + [vmem(table.shape, table.dtype) for table in tables]
        + [
            vmem((devices, 4, LANES), bf16),
            vmem((devices, 2, LANES), bf16),
            vmem((devices, 4, LANES), bf16),
            vmem((blocks, 2, LANES), bf16),
            vmem((devices, 2, LANES), bf16),
            vmem((blocks, 2, LANES), bf16),
            dma((3 + len(tables),)),
            dma(()),
            dma((groups,)),
            dma(()),
            dma(()),
            dma(()),
            dma(()),
            dma(()),
            dma(()),
        ],
        compiler_params=pltpu.CompilerParams(collective_id=0, has_side_effects=True),
    )(signal, cotangent, long_filter, *[jnp.asarray(table) for table in tables])
    gs_rows, gf_rows = (
        pltpu.with_memory_space_constraint(rows, pltpu.VMEM) for rows in (gs_rows, gf_rows)
    )
    result = jax.ShapeDtypeStruct((positions, columns), bf16)
    return pl.pallas_call(
        functools.partial(place_columns, columns // LANES),
        name="place_columns",
        out_shape=(result, result),
        in_specs=[whole] * 2,
        out_specs=(whole, whole),
    )(gs_rows, gf_rows)


def solution(mesh):
    in_specs = (P("cp", "tp"), P("cp", "tp"), P("cp", None))
    out_specs = (P("cp", "tp"), P("cp", None))
    run = functools.partial(body, mesh.shape["tp"], mesh.shape["cp"])
    return jax.shard_map(run, mesh=mesh, in_specs=in_specs, out_specs=out_specs, check_vma=False)
```

```python
import functools

import jax
import jax.numpy as jnp
import ml_dtypes
import numpy as np
from jax import lax
from jax.experimental import pallas as pl
from jax.experimental.pallas import tpu as pltpu
from jax.sharding import PartitionSpec as P

MESH = pl.DeviceIdType.MESH
bf16, f32 = jnp.bfloat16, jnp.float32
LANES = 128


def split_np(table):
    high = table.astype(ml_dtypes.bfloat16)
    low = (table - high.astype(np.float64)).astype(ml_dtypes.bfloat16)
    return high, low


def make_tables(blocks):
    half = 2 * blocks
    total = half * LANES
    w = np.arange(blocks) + 0.5
    k = np.arange(blocks)
    angle = 2 * np.pi * np.outer(w, k) / half
    pair = np.eye(2)
    cos_wk, sin_wk = np.kron(np.cos(angle), pair), np.kron(np.sin(angle), pair)
    filt = np.concatenate([cos_wk, -sin_wk], axis=0)
    both = np.zeros((2, 2, blocks, 2, blocks, 2, 2))
    for a in range(2):
        for c in range(2):
            both[a, 0, :, c, :, a, c] = np.cos(angle)
            both[a, 1, :, c, :, a, c] = -np.sin(angle)
    both = both.reshape(8 * blocks, 4 * blocks)
    lane = np.arange(LANES)
    twist = 2 * np.pi * np.outer(np.repeat(w, 2), lane) / total
    turn = 2 * np.pi * np.outer(lane, lane) / LANES
    cos_t, sin_t = np.cos(turn), np.sin(turn)
    forward = np.block([[cos_t, -sin_t], [sin_t, cos_t]])
    back = np.concatenate([cos_wk.T, -sin_wk.T], axis=1) * (2.0 / total)
    both_h, both_l = split_np(both)
    filt_h, filt_l = split_np(filt)
    forw_h, forw_l = split_np(forward)
    inv_h, inv_l = split_np(forward.T)
    back_h, back_l = split_np(back)
    tables = (
        np.concatenate([both_h, both_l], axis=1),
        np.concatenate([filt_h, filt_l], axis=1),
        np.stack([np.cos(twist), np.sin(twist)]).astype(np.float32),
        np.stack([forw_h, forw_l]),
        np.stack([inv_h, inv_l]),
        np.concatenate([back_h, back_h, back_l], axis=1),
    )
    return tables


def permutation(groups):
    table = np.zeros((groups, 2, 2, 2, groups, 2), np.float32)
    for d in range(groups):
        for a in range(2):
            for c in range(2):
                table[d, a, c, a, d, c] = 1
    return table.reshape(4 * groups, 4 * groups)


def dot(left, right):
    return lax.dot_general(left, right, (((1,), (0,)), ((), ())), preferred_element_type=f32)


def dot_nt(left, right):
    return lax.dot_general(left, right, (((1,), (1,)), ((), ())), preferred_element_type=f32)


def split(value):
    high = value.astype(bf16)
    low = (value - high.astype(f32)).astype(bf16)
    return high, low


def dot3(value, table_ref):
    high, low = split(value)
    top, bottom = table_ref[0], table_ref[1]
    return dot(high, top) + (dot(low, top) + dot(high, bottom))


def far_first(size):
    return sorted(range(size), key=lambda o: -min(o, size - o))


def exchange(groups, blocks, sig_hbm, cot_hbm, fil_hbm, *refs):
    tables_hbm, rest = refs[:7], refs[7:]
    out_gs, out_gf = rest[:2]
    sig, cot, fil = rest[2:5]
    both, filt, twist, forw, inv, back, perm = rest[5:12]
    (send, send_f, recv, recv_f, ready, ready_f) = rest[12:18]
    (load_sem, send_sem, recv_sem, send_f_sem, recv_f_sem) = rest[18:23]
    (gs_out_sem, gs_in_sem, gf_out_sem, gf_in_sem) = rest[23:]
    t = lax.axis_index("tp")
    p = lax.axis_index("cp")
    me = t * blocks + p
    devices = groups * blocks
    xs, lows = groups // 2, blocks // 8
    x, high = t // 2, lax.rem(t, 2)
    z, rest_p = high * lows + p // 8, lax.rem(p, 8)

    def greet_all():
        barrier = pltpu.get_barrier_semaphore()
        for z_off in far_first(2 * lows):
            z_to = lax.rem(z + z_off, 2 * lows)
            for x_off in far_first(xs):
                group = lax.rem(x + x_off, xs) * 2 + z_to // lows
                base = lax.rem(z_to, lows) * 8

                def greet(i, _, group=group, base=base):
                    place = base + lax.rem(rest_p + i, 8)
                    pl.semaphore_signal(
                        barrier, inc=1, device_id=(group, place), device_id_type=MESH
                    )
                    return 0

                lax.fori_loop(
                    1 if z_off == 0 and x_off == 0 else 0, 8, greet, 0, unroll=True
                )

    steps = [(x_off, h_off) for x_off in far_first(xs) for h_off in (1, 0)]
    steps = sorted(steps, key=lambda o: -min(o[0], xs - o[0]) - 0.5 * o[1])
    sizes = (groups // 2, groups // 2)

    def there(step):
        return lax.rem(x + step[0], xs) * 2 + lax.rem(high + step[1], 2)

    def origin(step):
        return lax.rem(x + xs - step[0], xs) * 2 + lax.rem(high + step[1], 2)

    def places(step, act):
        def one(i, _):
            act(lax.rem(p + i, blocks))
            return 0

        lax.fori_loop(1 if step == (0, 0) else 0, blocks, one, 0, unroll=8)

    loads = [
        pltpu.make_async_copy(source, target, load_sem.at[i])
        for i, (source, target) in enumerate(
            zip(
                (sig_hbm, cot_hbm, fil_hbm) + tuple(tables_hbm),
                (sig, cot, fil, both, filt, twist, forw, inv, back, perm),
                strict=True,
            )
        )
    ]
    for load in loads:
        load.start()
    greet_all()
    for load in loads:
        load.wait()

    eye = identity()
    per = LANES // 2
    for q in range(2 * devices // LANES):
        cols = pl.ds(q * LANES, LANES)
        pair = jnp.concatenate([sig[:, cols], cot[:, cols]], axis=1)
        moved = dot_nt(perm[...], pair)
        send[pl.ds(q * per, per)] = moved.reshape(per, 4, LANES).astype(bf16)
        moved = dot_nt(eye, fil[:, cols])
        send_f[pl.ds(q * per, per)] = moved.reshape(per, 2, LANES).astype(bf16)

    pl.semaphore_wait(pltpu.get_barrier_semaphore(), devices - 1)

    pltpu.make_async_copy(send_f.at[me], recv_f.at[p], recv_f_sem).start()

    def give_filter(place):
        pltpu.make_async_remote_copy(
            send_f.at[t * blocks + place],
            recv_f.at[p],
            send_f_sem,
            recv_f_sem,
            device_id=(t, place),
            device_id_type=MESH,
        ).start()

    for n, step in enumerate(steps):
        if n == len(steps) // 2:
            places((0, 0), give_filter)
        group = there(step)

        def give(place, n=n, group=group):
            pltpu.make_async_remote_copy(
                send.at[group * blocks + place],
                recv.at[me],
                send_sem,
                recv_sem.at[n],
                device_id=(group, place),
                device_id_type=MESH,
            ).start()

        places(step, give)
        if tuple(step) == (0, 0):
            pltpu.make_async_copy(send.at[me], recv.at[me], recv_sem.at[n]).start()

    turn_c, turn_s = twist[0], twist[1]
    width = 2 * blocks

    def turn(real, imag):
        return jnp.concatenate(
            [real * turn_c + imag * turn_s, imag * turn_c - real * turn_s], axis=1
        )

    def unturn(part):
        g_real, g_imag = part[:, :LANES], part[:, LANES:]
        return jnp.concatenate(
            [g_real * turn_c - g_imag * turn_s, g_real * turn_s + g_imag * turn_c], axis=0
        )

    def inverse(spectra):
        part = dot3(
            jnp.concatenate([jnp.concatenate(pair, axis=1) for pair in spectra], axis=0), inv
        )
        turned = [unturn(part[i * width : (i + 1) * width]) for i in range(len(spectra))]
        results = []
        for i in range(0, len(turned), 2):
            some = turned[i : i + 2]
            high_part, low_part = split(jnp.concatenate(some, axis=1))
            rows = dot(back[...], jnp.concatenate([high_part, low_part, high_part], axis=0))
            for n in range(len(some)):
                result = rows[:, n * LANES : (n + 1) * LANES]
                results.append(result.reshape(blocks, 2, LANES).astype(bf16))
        return results

    def give_rows(step):
        group = origin(step)

        def give_back(place):
            pltpu.make_async_remote_copy(
                ready.at[group * blocks + place],
                out_gs.at[me],
                gs_out_sem,
                gs_in_sem,
                device_id=(group, place),
                device_id_type=MESH,
            ).start()

        places(step, give_back)
        if step == (0, 0):
            pltpu.make_async_copy(ready.at[me], out_gs.at[me], gs_in_sem).start()

    def give_sums(step):
        group = origin(step)

        def give_last(place):
            pltpu.make_async_remote_copy(
                ready_f.at[place],
                out_gf.at[me],
                gf_out_sem,
                gf_in_sem,
                device_id=(group, place),
                device_id_type=MESH,
            ).start()

        places(step, give_last)
        if step == (0, 0):
            pltpu.make_async_copy(ready_f.at[p], out_gf.at[me], gf_in_sem).start()

    pltpu.make_async_copy(recv_f, recv_f, recv_f_sem).wait()
    data = recv_f[...].reshape(2 * blocks, LANES)
    halves = dot(filt[...], jnp.concatenate([data, data], axis=0))
    h_spec = dot3(turn(halves[:width], halves[width:]), forw)
    h_real, h_imag = h_spec[:, :LANES], h_spec[:, LANES:]

    sum_real = jnp.zeros((width, LANES), f32)
    sum_imag = jnp.zeros((width, LANES), f32)
    first = 0
    for size in sizes:
        some = range(first, first + size)
        first += size
        mine = [pl.ds(origin(steps[n]) * blocks, blocks) for n in some]
        for n, rows in zip(some, mine, strict=True):
            pltpu.make_async_copy(recv.at[rows], recv.at[rows], recv_sem.at[n]).wait()
        turned = []
        for i in range(0, size, 2):
            data = jnp.concatenate(
                [recv[rows].reshape(4 * blocks, LANES) for rows in mine[i : i + 2]], axis=1
            )
            halves = dot(both[...], jnp.concatenate([data, data], axis=0))
            for n in range(len(mine[i : i + 2])):
                part = halves[:, n * LANES : (n + 1) * LANES]
                turned.append(turn(part[:width], part[width : 2 * width]))
                turned.append(turn(part[2 * width : 3 * width], part[3 * width :]))
        spec = dot3(jnp.concatenate(turned, axis=0), forw)
        products = []
        for n in range(size):
            u_spec = spec[2 * n * width : (2 * n + 1) * width]
            d_spec = spec[(2 * n + 1) * width : (2 * n + 2) * width]
            u_real, u_imag = u_spec[:, :LANES], u_spec[:, LANES:]
            d_real, d_imag = d_spec[:, :LANES], d_spec[:, LANES:]
            sum_real = sum_real + (u_real * d_real + u_imag * d_imag)
            sum_imag = sum_imag + (u_real * d_imag - u_imag * d_real)
            products.append(
                (h_real * d_real + h_imag * d_imag, h_real * d_imag - h_imag * d_real)
            )
        if first == len(steps):
            products.append((sum_real, sum_imag))
        results = inverse(products)
        if first == len(steps):
            ready_f[...] = results[-1]
            for step in steps:
                give_sums(step)
        for rows, result in zip(mine, results[:size], strict=True):
            ready[rows] = result
        for n in some:
            give_rows(steps[n])

    some = pl.ds(0, devices - 1)
    pltpu.make_async_copy(send.at[some], send.at[some], send_sem).wait()
    pltpu.make_async_copy(ready.at[some], ready.at[some], gs_out_sem).wait()
    few = pl.ds(0, blocks - 1)
    pltpu.make_async_copy(send_f.at[few], send_f.at[few], send_f_sem).wait()
    pltpu.make_async_copy(out_gf.at[some], out_gf.at[some], gf_out_sem).wait()
    pltpu.make_async_copy(out_gs, out_gs, gs_in_sem).wait()
    pltpu.make_async_copy(out_gf, out_gf, gf_in_sem).wait()


def identity():
    rows = lax.broadcasted_iota(jnp.int32, (LANES, LANES), 0)
    cols = lax.broadcasted_iota(jnp.int32, (LANES, LANES), 1)
    return (rows == cols).astype(f32).astype(bf16)


def place_columns(quarters, gs_in, gf_in, gs_ref, gf_ref):
    eye = identity()
    per = LANES // 2
    for q in range(quarters):
        for source, target in ((gs_in, gs_ref), (gf_in, gf_ref)):
            block = source[pl.ds(q * per, per)].reshape(LANES, LANES)
            target[:, pl.ds(q * LANES, LANES)] = dot_nt(eye, block).astype(bf16)


def body(groups, blocks, signal, cotangent, long_filter):
    positions, columns = signal.shape
    devices = groups * blocks
    tables = make_tables(blocks) + (permutation(LANES // 2).astype(ml_dtypes.bfloat16),)
    vmem = pltpu.VMEM
    dma = pltpu.SemaphoreType.DMA
    anywhere = pl.BlockSpec(memory_space=pl.ANY)
    whole = pl.BlockSpec(memory_space=pltpu.VMEM)
    pairs = pltpu.VMEM((devices, 2, LANES), bf16)
    gs_rows, gf_rows = pl.pallas_call(
        functools.partial(exchange, groups, blocks),
        name="exchange",
        out_shape=(pairs, pairs),
        in_specs=[anywhere] * (3 + len(tables)),
        out_specs=(whole, whole),
        scratch_shapes=[vmem((positions, columns), bf16)] * 3
        + [vmem(table.shape, table.dtype) for table in tables]
        + [
            vmem((devices, 4, LANES), bf16),
            vmem((devices, 2, LANES), bf16),
            vmem((devices, 4, LANES), bf16),
            vmem((blocks, 2, LANES), bf16),
            vmem((devices, 2, LANES), bf16),
            vmem((blocks, 2, LANES), bf16),
            dma((3 + len(tables),)),
            dma(()),
            dma((groups,)),
            dma(()),
            dma(()),
            dma(()),
            dma(()),
            dma(()),
            dma(()),
        ],
        compiler_params=pltpu.CompilerParams(collective_id=0, has_side_effects=True),
    )(signal, cotangent, long_filter, *[jnp.asarray(table) for table in tables])
    gs_rows, gf_rows = (
        pltpu.with_memory_space_constraint(rows, pltpu.VMEM) for rows in (gs_rows, gf_rows)
    )
    result = jax.ShapeDtypeStruct((positions, columns), bf16)
    return pl.pallas_call(
        functools.partial(place_columns, columns // LANES),
        name="place_columns",
        out_shape=(result, result),
        in_specs=[whole] * 2,
        out_specs=(whole, whole),
    )(gs_rows, gf_rows)


def solution(mesh):
    in_specs = (P("cp", "tp"), P("cp", "tp"), P("cp", None))
    out_specs = (P("cp", "tp"), P("cp", None))
    run = functools.partial(body, mesh.shape["tp"], mesh.shape["cp"])
    return jax.shard_map(run, mesh=mesh, in_specs=in_specs, out_specs=out_specs, check_vma=False)
```

```python
import functools

import jax
import jax.numpy as jnp
import ml_dtypes
import numpy as np
from jax import lax
from jax.experimental import pallas as pl
from jax.experimental.pallas import tpu as pltpu
from jax.sharding import PartitionSpec as P

MESH = pl.DeviceIdType.MESH
bf16, f32 = jnp.bfloat16, jnp.float32
LANES = 128


def split_np(table):
    high = table.astype(ml_dtypes.bfloat16)
    low = (table - high.astype(np.float64)).astype(ml_dtypes.bfloat16)
    return high, low


def make_tables(blocks):
    half = 2 * blocks
    total = half * LANES
    w = np.arange(blocks) + 0.5
    k = np.arange(blocks)
    angle = 2 * np.pi * np.outer(w, k) / half
    pair = np.eye(2)
    cos_wk, sin_wk = np.kron(np.cos(angle), pair), np.kron(np.sin(angle), pair)
    filt = np.concatenate([cos_wk, -sin_wk], axis=0)
    both = np.zeros((2, 2, blocks, 2, blocks, 2, 2))
    for a in range(2):
        for c in range(2):
            both[a, 0, :, c, :, a, c] = np.cos(angle)
            both[a, 1, :, c, :, a, c] = -np.sin(angle)
    both = both.reshape(8 * blocks, 4 * blocks)
    lane = np.arange(LANES)
    twist = 2 * np.pi * np.outer(np.repeat(w, 2), lane) / total
    turn = 2 * np.pi * np.outer(lane, lane) / LANES
    cos_t, sin_t = np.cos(turn), np.sin(turn)
    forward = np.block([[cos_t, -sin_t], [sin_t, cos_t]])
    back = np.concatenate([cos_wk.T, -sin_wk.T], axis=1) * (2.0 / total)
    both_h, both_l = split_np(both)
    filt_h, filt_l = split_np(filt)
    forw_h, forw_l = split_np(forward)
    inv_h, inv_l = split_np(forward.T)
    back_h, back_l = split_np(back)
    tables = (
        np.concatenate([both_h, both_l], axis=1),
        np.concatenate([filt_h, filt_l], axis=1),
        np.stack([np.cos(twist), np.sin(twist)]).astype(np.float32),
        np.stack([forw_h, forw_l]),
        np.stack([inv_h, inv_l]),
        np.concatenate([back_h, back_h, back_l], axis=1),
    )
    return tables


def permutation(groups):
    table = np.zeros((groups, 2, 2, 2, groups, 2), np.float32)
    for d in range(groups):
        for a in range(2):
            for c in range(2):
                table[d, a, c, a, d, c] = 1
    return table.reshape(4 * groups, 4 * groups)


def dot(left, right):
    return lax.dot_general(left, right, (((1,), (0,)), ((), ())), preferred_element_type=f32)


def dot_nt(left, right):
    return lax.dot_general(left, right, (((1,), (1,)), ((), ())), preferred_element_type=f32)


def split(value):
    high = value.astype(bf16)
    low = (value - high.astype(f32)).astype(bf16)
    return high, low


def dot3(value, table_ref):
    high, low = split(value)
    top, bottom = table_ref[0], table_ref[1]
    return dot(high, top) + (dot(low, top) + dot(high, bottom))


def far_first(size):
    return sorted(range(size), key=lambda o: -min(o, size - o))


def exchange(groups, blocks, sig_hbm, cot_hbm, fil_hbm, *refs):
    tables_hbm, rest = refs[:7], refs[7:]
    out_gs, out_gf = rest[:2]
    sig, cot, fil = rest[2:5]
    both, filt, twist, forw, inv, back, perm = rest[5:12]
    (send, send_f, recv, recv_f, ready, ready_f) = rest[12:18]
    (load_sem, send_sem, recv_sem, send_f_sem, recv_f_sem) = rest[18:23]
    (gs_out_sem, gs_in_sem, gf_out_sem, gf_in_sem) = rest[23:]
    t = lax.axis_index("tp")
    p = lax.axis_index("cp")
    me = t * blocks + p
    devices = groups * blocks
    xs, lows = groups // 2, blocks // 8
    x, high = t // 2, lax.rem(t, 2)
    z, rest_p = high * lows + p // 8, lax.rem(p, 8)

    def greet_all():
        barrier = pltpu.get_barrier_semaphore()
        for z_off in far_first(2 * lows):
            z_to = lax.rem(z + z_off, 2 * lows)
            for x_off in far_first(xs):
                group = lax.rem(x + x_off, xs) * 2 + z_to // lows
                base = lax.rem(z_to, lows) * 8

                def greet(i, _, group=group, base=base):
                    place = base + lax.rem(rest_p + i, 8)
                    pl.semaphore_signal(
                        barrier, inc=1, device_id=(group, place), device_id_type=MESH
                    )
                    return 0

                lax.fori_loop(
                    1 if z_off == 0 and x_off == 0 else 0, 8, greet, 0, unroll=True
                )

    steps = [(x_off, h_off) for x_off in far_first(xs) for h_off in (1, 0)]
    steps = sorted(steps, key=lambda o: -min(o[0], xs - o[0]) - 0.5 * o[1])
    sizes = (groups // 4, groups // 4, groups // 2)

    def there(step):
        return lax.rem(x + step[0], xs) * 2 + lax.rem(high + step[1], 2)

    def origin(step):
        return lax.rem(x + xs - step[0], xs) * 2 + lax.rem(high + step[1], 2)

    def places(step, act):
        def one(i, _):
            act(lax.rem(p + i, blocks))
            return 0

        lax.fori_loop(1 if step == (0, 0) else 0, blocks, one, 0, unroll=8)

    loads = [
        pltpu.make_async_copy(source, target, load_sem.at[i])
        for i, (source, target) in enumerate(
            zip(
                (sig_hbm, cot_hbm, fil_hbm) + tuple(tables_hbm),
                (sig, cot, fil, both, filt, twist, forw, inv, back, perm),
                strict=True,
            )
        )
    ]
    for load in loads:
        load.start()
    greet_all()
    for load in loads:
        load.wait()

    eye = identity()
    per = LANES // 2
    for q in range(2 * devices // LANES):
        cols = pl.ds(q * LANES, LANES)
        pair = jnp.concatenate([sig[:, cols], cot[:, cols]], axis=1)
        moved = dot_nt(perm[...], pair)
        send[pl.ds(q * per, per)] = moved.reshape(per, 4, LANES).astype(bf16)
        moved = dot_nt(eye, fil[:, cols])
        send_f[pl.ds(q * per, per)] = moved.reshape(per, 2, LANES).astype(bf16)

    pl.semaphore_wait(pltpu.get_barrier_semaphore(), devices - 1)

    pltpu.make_async_copy(send_f.at[me], recv_f.at[p], recv_f_sem).start()

    def give_filter(place):
        pltpu.make_async_remote_copy(
            send_f.at[t * blocks + place],
            recv_f.at[p],
            send_f_sem,
            recv_f_sem,
            device_id=(t, place),
            device_id_type=MESH,
        ).start()

    for n, step in enumerate(steps):
        if n == len(steps) // 4:
            places((0, 0), give_filter)
        group = there(step)

        def give(place, n=n, group=group):
            pltpu.make_async_remote_copy(
                send.at[group * blocks + place],
                recv.at[me],
                send_sem,
                recv_sem.at[n],
                device_id=(group, place),
                device_id_type=MESH,
            ).start()

        places(step, give)
        if tuple(step) == (0, 0):
            pltpu.make_async_copy(send.at[me], recv.at[me], recv_sem.at[n]).start()

    turn_c, turn_s = twist[0], twist[1]
    width = 2 * blocks

    def turn(real, imag):
        return jnp.concatenate(
            [real * turn_c + imag * turn_s, imag * turn_c - real * turn_s], axis=1
        )

    def unturn(part):
        g_real, g_imag = part[:, :LANES], part[:, LANES:]
        return jnp.concatenate(
            [g_real * turn_c - g_imag * turn_s, g_real * turn_s + g_imag * turn_c], axis=0
        )

    def inverse(spectra):
        part = dot3(
            jnp.concatenate([jnp.concatenate(pair, axis=1) for pair in spectra], axis=0), inv
        )
        turned = [unturn(part[i * width : (i + 1) * width]) for i in range(len(spectra))]
        results = []
        for i in range(0, len(turned), 2):
            some = turned[i : i + 2]
            high_part, low_part = split(jnp.concatenate(some, axis=1))
            rows = dot(back[...], jnp.concatenate([high_part, low_part, high_part], axis=0))
            for n in range(len(some)):
                result = rows[:, n * LANES : (n + 1) * LANES]
                results.append(result.reshape(blocks, 2, LANES).astype(bf16))
        return results

    def give_rows(step):
        group = origin(step)

        def give_back(place):
            pltpu.make_async_remote_copy(
                ready.at[group * blocks + place],
                out_gs.at[me],
                gs_out_sem,
                gs_in_sem,
                device_id=(group, place),
                device_id_type=MESH,
            ).start()

        places(step, give_back)
        if step == (0, 0):
            pltpu.make_async_copy(ready.at[me], out_gs.at[me], gs_in_sem).start()

    def give_sums(half):
        for x_off in far_first(xs):
            group = lax.rem(x + xs - x_off, xs) * 2 + half

            def give_last(i, _, group=group):
                place = lax.rem(p + i, blocks)
                pltpu.make_async_remote_copy(
                    ready_f.at[place],
                    out_gf.at[me],
                    gf_out_sem,
                    gf_in_sem,
                    device_id=(group, place),
                    device_id_type=MESH,
                ).start()
                return 0

            if x_off == 0:
                @pl.when(group != t)
                def _():
                    give_last(0, 0)
            else:
                give_last(0, 0)
            lax.fori_loop(1, blocks, give_last, 0, unroll=8)

    pltpu.make_async_copy(recv_f, recv_f, recv_f_sem).wait()
    data = recv_f[...].reshape(2 * blocks, LANES)
    halves = dot(filt[...], jnp.concatenate([data, data], axis=0))
    h_spec = dot3(turn(halves[:width], halves[width:]), forw)
    h_real, h_imag = h_spec[:, :LANES], h_spec[:, LANES:]

    sum_real = jnp.zeros((width, LANES), f32)
    sum_imag = jnp.zeros((width, LANES), f32)
    first = 0
    for size in sizes:
        some = range(first, first + size)
        first += size
        mine = [pl.ds(origin(steps[n]) * blocks, blocks) for n in some]
        for n, rows in zip(some, mine, strict=True):
            pltpu.make_async_copy(recv.at[rows], recv.at[rows], recv_sem.at[n]).wait()
        turned = []
        for i in range(0, size, 2):
            data = jnp.concatenate(
                [recv[rows].reshape(4 * blocks, LANES) for rows in mine[i : i + 2]], axis=1
            )
            halves = dot(both[...], jnp.concatenate([data, data], axis=0))
            for n in range(len(mine[i : i + 2])):
                part = halves[:, n * LANES : (n + 1) * LANES]
                turned.append(turn(part[:width], part[width : 2 * width]))
                turned.append(turn(part[2 * width : 3 * width], part[3 * width :]))
        spec = dot3(jnp.concatenate(turned, axis=0), forw)
        products = []
        for n in range(size):
            u_spec = spec[2 * n * width : (2 * n + 1) * width]
            d_spec = spec[(2 * n + 1) * width : (2 * n + 2) * width]
            u_real, u_imag = u_spec[:, :LANES], u_spec[:, LANES:]
            d_real, d_imag = d_spec[:, :LANES], d_spec[:, LANES:]
            sum_real = sum_real + (u_real * d_real + u_imag * d_imag)
            sum_imag = sum_imag + (u_real * d_imag - u_imag * d_real)
            products.append(
                (h_real * d_real + h_imag * d_imag, h_real * d_imag - h_imag * d_real)
            )
        if first == len(steps):
            products.append((sum_real, sum_imag))
        results = inverse(products)
        if first == len(steps):
            ready_f[...] = results[-1]
            pltpu.make_async_copy(ready_f.at[p], out_gf.at[me], gf_in_sem).start()
            give_sums(0)
        for rows, result in zip(mine, results[:size], strict=True):
            ready[rows] = result
        for n in sorted(some, key=lambda n: -steps[n][1]):
            give_rows(steps[n])
    give_sums(1)

    some = pl.ds(0, devices - 1)
    pltpu.make_async_copy(send.at[some], send.at[some], send_sem).wait()
    pltpu.make_async_copy(ready.at[some], ready.at[some], gs_out_sem).wait()
    few = pl.ds(0, blocks - 1)
    pltpu.make_async_copy(send_f.at[few], send_f.at[few], send_f_sem).wait()
    pltpu.make_async_copy(out_gf.at[some], out_gf.at[some], gf_out_sem).wait()
    pltpu.make_async_copy(out_gs, out_gs, gs_in_sem).wait()
    pltpu.make_async_copy(out_gf, out_gf, gf_in_sem).wait()


def identity():
    rows = lax.broadcasted_iota(jnp.int32, (LANES, LANES), 0)
    cols = lax.broadcasted_iota(jnp.int32, (LANES, LANES), 1)
    return (rows == cols).astype(f32).astype(bf16)


def place_columns(quarters, gs_in, gf_in, gs_ref, gf_ref):
    eye = identity()
    per = LANES // 2
    for q in range(quarters):
        for source, target in ((gs_in, gs_ref), (gf_in, gf_ref)):
            block = source[pl.ds(q * per, per)].reshape(LANES, LANES)
            target[:, pl.ds(q * LANES, LANES)] = dot_nt(eye, block).astype(bf16)


def body(groups, blocks, signal, cotangent, long_filter):
    positions, columns = signal.shape
    devices = groups * blocks
    tables = make_tables(blocks) + (permutation(LANES // 2).astype(ml_dtypes.bfloat16),)
    vmem = pltpu.VMEM
    dma = pltpu.SemaphoreType.DMA
    anywhere = pl.BlockSpec(memory_space=pl.ANY)
    whole = pl.BlockSpec(memory_space=pltpu.VMEM)
    pairs = pltpu.VMEM((devices, 2, LANES), bf16)
    gs_rows, gf_rows = pl.pallas_call(
        functools.partial(exchange, groups, blocks),
        name="exchange",
        out_shape=(pairs, pairs),
        in_specs=[anywhere] * (3 + len(tables)),
        out_specs=(whole, whole),
        scratch_shapes=[vmem((positions, columns), bf16)] * 3
        + [vmem(table.shape, table.dtype) for table in tables]
        + [
            vmem((devices, 4, LANES), bf16),
            vmem((devices, 2, LANES), bf16),
            vmem((devices, 4, LANES), bf16),
            vmem((blocks, 2, LANES), bf16),
            vmem((devices, 2, LANES), bf16),
            vmem((blocks, 2, LANES), bf16),
            dma((3 + len(tables),)),
            dma(()),
            dma((groups,)),
            dma(()),
            dma(()),
            dma(()),
            dma(()),
            dma(()),
            dma(()),
        ],
        compiler_params=pltpu.CompilerParams(collective_id=0, has_side_effects=True),
    )(signal, cotangent, long_filter, *[jnp.asarray(table) for table in tables])
    gs_rows, gf_rows = (
        pltpu.with_memory_space_constraint(rows, pltpu.VMEM) for rows in (gs_rows, gf_rows)
    )
    result = jax.ShapeDtypeStruct((positions, columns), bf16)
    return pl.pallas_call(
        functools.partial(place_columns, columns // LANES),
        name="place_columns",
        out_shape=(result, result),
        in_specs=[whole] * 2,
        out_specs=(whole, whole),
    )(gs_rows, gf_rows)


def solution(mesh):
    in_specs = (P("cp", "tp"), P("cp", "tp"), P("cp", None))
    out_specs = (P("cp", "tp"), P("cp", None))
    run = functools.partial(body, mesh.shape["tp"], mesh.shape["cp"])
    return jax.shard_map(run, mesh=mesh, in_specs=in_specs, out_specs=out_specs, check_vma=False)
```

```python
import functools

import jax
import jax.numpy as jnp
import ml_dtypes
import numpy as np
from jax import lax
from jax.experimental import pallas as pl
from jax.experimental.pallas import tpu as pltpu
from jax.sharding import PartitionSpec as P

MESH = pl.DeviceIdType.MESH
bf16, f32 = jnp.bfloat16, jnp.float32
LANES = 128


def split_np(table):
    high = table.astype(ml_dtypes.bfloat16)
    low = (table - high.astype(np.float64)).astype(ml_dtypes.bfloat16)
    return high, low


def make_tables(blocks):
    half = 2 * blocks
    total = half * LANES
    w = np.arange(blocks) + 0.5
    k = np.arange(blocks)
    angle = 2 * np.pi * np.outer(w, k) / half
    pair = np.eye(2)
    cos_wk, sin_wk = np.kron(np.cos(angle), pair), np.kron(np.sin(angle), pair)
    filt = np.concatenate([cos_wk, -sin_wk], axis=0)
    both = np.zeros((2, 2, blocks, 2, blocks, 2, 2))
    for a in range(2):
        for c in range(2):
            both[a, 0, :, c, :, a, c] = np.cos(angle)
            both[a, 1, :, c, :, a, c] = -np.sin(angle)
    both = both.reshape(8 * blocks, 4 * blocks)
    lane = np.arange(LANES)
    twist = 2 * np.pi * np.outer(np.repeat(w, 2), lane) / total
    turn = 2 * np.pi * np.outer(lane, lane) / LANES
    cos_t, sin_t = np.cos(turn), np.sin(turn)
    forward = np.block([[cos_t, -sin_t], [sin_t, cos_t]])
    back = np.concatenate([cos_wk.T, -sin_wk.T], axis=1) * (2.0 / total)
    both_h, both_l = split_np(both)
    filt_h, filt_l = split_np(filt)
    forw_h, forw_l = split_np(forward)
    inv_h, inv_l = split_np(forward.T)
    back_h, back_l = split_np(back)
    tables = (
        np.concatenate([both_h, both_l], axis=1),
        np.concatenate([filt_h, filt_l], axis=1),
        np.stack([np.cos(twist), np.sin(twist)]).astype(np.float32),
        np.stack([forw_h, forw_l]),
        np.stack([inv_h, inv_l]),
        np.concatenate([back_h, back_h, back_l], axis=1),
    )
    return tables


def permutation(groups):
    table = np.zeros((groups, 2, 2, 2, groups, 2), np.float32)
    for d in range(groups):
        for a in range(2):
            for c in range(2):
                table[d, a, c, a, d, c] = 1
    return table.reshape(4 * groups, 4 * groups)


def dot(left, right):
    return lax.dot_general(left, right, (((1,), (0,)), ((), ())), preferred_element_type=f32)


def dot_nt(left, right):
    return lax.dot_general(left, right, (((1,), (1,)), ((), ())), preferred_element_type=f32)


def split(value):
    high = value.astype(bf16)
    low = (value - high.astype(f32)).astype(bf16)
    return high, low


def dot3(value, table_ref):
    high, low = split(value)
    top, bottom = table_ref[0], table_ref[1]
    return dot(high, top) + (dot(low, top) + dot(high, bottom))


def far_first(size):
    return sorted(range(size), key=lambda o: -min(o, size - o))


def exchange(groups, blocks, sig_hbm, cot_hbm, fil_hbm, *refs):
    tables_hbm, rest = refs[:7], refs[7:]
    out_gs, out_gf = rest[:2]
    sig, cot, fil = rest[2:5]
    both, filt, twist, forw, inv, back, perm = rest[5:12]
    (send, send_f, recv, recv_f, ready, ready_f) = rest[12:18]
    (load_sem, send_sem, recv_sem, send_f_sem, recv_f_sem) = rest[18:23]
    (gs_out_sem, gs_in_sem, gf_out_sem, gf_in_sem) = rest[23:]
    t = lax.axis_index("tp")
    p = lax.axis_index("cp")
    me = t * blocks + p
    devices = groups * blocks
    xs, lows = groups // 2, blocks // 8
    x, high = t // 2, lax.rem(t, 2)
    z, rest_p = high * lows + p // 8, lax.rem(p, 8)

    def greet_all(loads):
        barrier = pltpu.get_barrier_semaphore()
        for z_off in far_first(2 * lows):
            if z_off == lows - 2:
                for load in loads:
                    load.start()
            z_to = lax.rem(z + z_off, 2 * lows)
            for x_off in far_first(xs):
                group = lax.rem(x + x_off, xs) * 2 + z_to // lows
                base = lax.rem(z_to, lows) * 8

                def greet(i, _, group=group, base=base):
                    place = base + lax.rem(rest_p + i, 8)
                    pl.semaphore_signal(
                        barrier, inc=1, device_id=(group, place), device_id_type=MESH
                    )
                    return 0

                lax.fori_loop(
                    1 if z_off == 0 and x_off == 0 else 0, 8, greet, 0, unroll=True
                )

    steps = [(x_off, h_off) for x_off in far_first(xs) for h_off in (1, 0)]
    steps = sorted(steps, key=lambda o: -min(o[0], xs - o[0]) - 0.5 * o[1])
    sizes = (groups // 4, groups // 4, groups // 2)

    def there(step):
        return lax.rem(x + step[0], xs) * 2 + lax.rem(high + step[1], 2)

    def origin(step):
        return lax.rem(x + xs - step[0], xs) * 2 + lax.rem(high + step[1], 2)

    def places(step, act):
        def one(i, _):
            act(lax.rem(p + i, blocks))
            return 0

        lax.fori_loop(1 if step == (0, 0) else 0, blocks, one, 0, unroll=8)

    loads = [
        pltpu.make_async_copy(source, target, load_sem.at[i])
        for i, (source, target) in enumerate(
            zip(
                (sig_hbm, cot_hbm, fil_hbm) + tuple(tables_hbm),
                (sig, cot, fil, both, filt, twist, forw, inv, back, perm),
                strict=True,
            )
        )
    ]
    greet_all(loads)
    for load in loads:
        load.wait()

    eye = identity()
    per = LANES // 2
    for q in range(2 * devices // LANES):
        cols = pl.ds(q * LANES, LANES)
        pair = jnp.concatenate([sig[:, cols], cot[:, cols]], axis=1)
        moved = dot_nt(perm[...], pair)
        send[pl.ds(q * per, per)] = moved.reshape(per, 4, LANES).astype(bf16)
        moved = dot_nt(eye, fil[:, cols])
        send_f[pl.ds(q * per, per)] = moved.reshape(per, 2, LANES).astype(bf16)

    pl.semaphore_wait(pltpu.get_barrier_semaphore(), devices - 1)

    pltpu.make_async_copy(send_f.at[me], recv_f.at[p], recv_f_sem).start()

    def give_filter(place):
        pltpu.make_async_remote_copy(
            send_f.at[t * blocks + place],
            recv_f.at[p],
            send_f_sem,
            recv_f_sem,
            device_id=(t, place),
            device_id_type=MESH,
        ).start()

    for n, step in enumerate(steps):
        if n == len(steps) // 4:
            places((0, 0), give_filter)
        group = there(step)

        def give(place, n=n, group=group):
            pltpu.make_async_remote_copy(
                send.at[group * blocks + place],
                recv.at[me],
                send_sem,
                recv_sem.at[n],
                device_id=(group, place),
                device_id_type=MESH,
            ).start()

        places(step, give)
        if tuple(step) == (0, 0):
            pltpu.make_async_copy(send.at[me], recv.at[me], recv_sem.at[n]).start()

    turn_c, turn_s = twist[0], twist[1]
    width = 2 * blocks

    def turn(real, imag):
        return jnp.concatenate(
            [real * turn_c + imag * turn_s, imag * turn_c - real * turn_s], axis=1
        )

    def unturn(part):
        g_real, g_imag = part[:, :LANES], part[:, LANES:]
        return jnp.concatenate(
            [g_real * turn_c - g_imag * turn_s, g_real * turn_s + g_imag * turn_c], axis=0
        )

    def inverse(spectra):
        part = dot3(
            jnp.concatenate([jnp.concatenate(pair, axis=1) for pair in spectra], axis=0), inv
        )
        turned = [unturn(part[i * width : (i + 1) * width]) for i in range(len(spectra))]
        results = []
        for i in range(0, len(turned), 2):
            some = turned[i : i + 2]
            high_part, low_part = split(jnp.concatenate(some, axis=1))
            rows = dot(back[...], jnp.concatenate([high_part, low_part, high_part], axis=0))
            for n in range(len(some)):
                result = rows[:, n * LANES : (n + 1) * LANES]
                results.append(result.reshape(blocks, 2, LANES).astype(bf16))
        return results

    head = 1
    turn_to_head = lax.rem(head - p + blocks, blocks)

    def all_but_head(group, act):
        def one(i, _):
            act(lax.rem(p + i, blocks))
            return 0

        @pl.when(jnp.logical_and(group != t, p != head))
        def _():
            act(p)

        lax.fori_loop(1, turn_to_head, one, 0)
        lax.fori_loop(turn_to_head + 1, blocks, one, 0)

        @pl.when(jnp.logical_and(group != 0, jnp.logical_or(group != t, p != head)))
        def _():
            act(head)

    def give_row(group, place):
        pltpu.make_async_remote_copy(
            ready.at[group * blocks + place],
            out_gs.at[me],
            gs_out_sem,
            gs_in_sem,
            device_id=(group, place),
            device_id_type=MESH,
        ).start()

    def give_rows(step, late):
        group = origin(step)
        if late:
            all_but_head(group, functools.partial(give_row, group))
        else:
            places(step, functools.partial(give_row, group))
        if step == (0, 0):
            pltpu.make_async_copy(ready.at[me], out_gs.at[me], gs_in_sem).start()

    def give_sum(group, place):
        pltpu.make_async_remote_copy(
            ready_f.at[place],
            out_gf.at[me],
            gf_out_sem,
            gf_in_sem,
            device_id=(group, place),
            device_id_type=MESH,
        ).start()

    def give_sums(half):
        for x_off in far_first(xs):
            group = lax.rem(x + xs - x_off, xs) * 2 + half
            all_but_head(group, functools.partial(give_sum, group))

    pltpu.make_async_copy(recv_f, recv_f, recv_f_sem).wait()
    data = recv_f[...].reshape(2 * blocks, LANES)
    halves = dot(filt[...], jnp.concatenate([data, data], axis=0))
    h_spec = dot3(turn(halves[:width], halves[width:]), forw)
    h_real, h_imag = h_spec[:, :LANES], h_spec[:, LANES:]

    sum_real = jnp.zeros((width, LANES), f32)
    sum_imag = jnp.zeros((width, LANES), f32)
    first = 0
    for size in sizes:
        some = range(first, first + size)
        first += size
        mine = [pl.ds(origin(steps[n]) * blocks, blocks) for n in some]
        for n, rows in zip(some, mine, strict=True):
            pltpu.make_async_copy(recv.at[rows], recv.at[rows], recv_sem.at[n]).wait()
        turned = []
        for i in range(0, size, 2):
            data = jnp.concatenate(
                [recv[rows].reshape(4 * blocks, LANES) for rows in mine[i : i + 2]], axis=1
            )
            halves = dot(both[...], jnp.concatenate([data, data], axis=0))
            for n in range(len(mine[i : i + 2])):
                part = halves[:, n * LANES : (n + 1) * LANES]
                turned.append(turn(part[:width], part[width : 2 * width]))
                turned.append(turn(part[2 * width : 3 * width], part[3 * width :]))
        spec = dot3(jnp.concatenate(turned, axis=0), forw)
        products = []
        for n in range(size):
            u_spec = spec[2 * n * width : (2 * n + 1) * width]
            d_spec = spec[(2 * n + 1) * width : (2 * n + 2) * width]
            u_real, u_imag = u_spec[:, :LANES], u_spec[:, LANES:]
            d_real, d_imag = d_spec[:, :LANES], d_spec[:, LANES:]
            sum_real = sum_real + (u_real * d_real + u_imag * d_imag)
            sum_imag = sum_imag + (u_real * d_imag - u_imag * d_real)
            products.append(
                (h_real * d_real + h_imag * d_imag, h_real * d_imag - h_imag * d_real)
            )
        if first == len(steps):
            products.append((sum_real, sum_imag))
        results = inverse(products)
        late = first == len(steps)
        if late:
            ready_f[...] = results[-1]
        for rows, result in zip(mine, results[:size], strict=True):
            ready[rows] = result
        if late:
            pltpu.make_async_copy(ready_f.at[p], out_gf.at[me], gf_in_sem).start()

            @pl.when(me != head)
            def _():
                give_sum(0, head)

            for n in some:

                @pl.when(jnp.logical_and(origin(steps[n]) == 0, me != head))
                def _():
                    give_row(0, head)

            give_sums(0)
        for n in sorted(some, key=lambda n: -steps[n][1]):
            give_rows(steps[n], late)
    give_sums(1)

    some = pl.ds(0, devices - 1)
    pltpu.make_async_copy(send.at[some], send.at[some], send_sem).wait()
    pltpu.make_async_copy(ready.at[some], ready.at[some], gs_out_sem).wait()
    few = pl.ds(0, blocks - 1)
    pltpu.make_async_copy(send_f.at[few], send_f.at[few], send_f_sem).wait()
    pltpu.make_async_copy(out_gf.at[some], out_gf.at[some], gf_out_sem).wait()
    pltpu.make_async_copy(out_gs, out_gs, gs_in_sem).wait()
    pltpu.make_async_copy(out_gf, out_gf, gf_in_sem).wait()


def identity():
    rows = lax.broadcasted_iota(jnp.int32, (LANES, LANES), 0)
    cols = lax.broadcasted_iota(jnp.int32, (LANES, LANES), 1)
    return (rows == cols).astype(f32).astype(bf16)


def place_columns(quarters, gs_in, gf_in, gs_ref, gf_ref):
    eye = identity()
    per = LANES // 2
    for q in range(quarters):
        for source, target in ((gs_in, gs_ref), (gf_in, gf_ref)):
            block = source[pl.ds(q * per, per)].reshape(LANES, LANES)
            target[:, pl.ds(q * LANES, LANES)] = dot_nt(eye, block).astype(bf16)


def body(groups, blocks, signal, cotangent, long_filter):
    positions, columns = signal.shape
    devices = groups * blocks
    tables = make_tables(blocks) + (permutation(LANES // 2).astype(ml_dtypes.bfloat16),)
    vmem = pltpu.VMEM
    dma = pltpu.SemaphoreType.DMA
    anywhere = pl.BlockSpec(memory_space=pl.ANY)
    whole = pl.BlockSpec(memory_space=pltpu.VMEM)
    pairs = pltpu.VMEM((devices, 2, LANES), bf16)
    gs_rows, gf_rows = pl.pallas_call(
        functools.partial(exchange, groups, blocks),
        name="exchange",
        out_shape=(pairs, pairs),
        in_specs=[anywhere] * (3 + len(tables)),
        out_specs=(whole, whole),
        scratch_shapes=[vmem((positions, columns), bf16)] * 3
        + [vmem(table.shape, table.dtype) for table in tables]
        + [
            vmem((devices, 4, LANES), bf16),
            vmem((devices, 2, LANES), bf16),
            vmem((devices, 4, LANES), bf16),
            vmem((blocks, 2, LANES), bf16),
            vmem((devices, 2, LANES), bf16),
            vmem((blocks, 2, LANES), bf16),
            dma((3 + len(tables),)),
            dma(()),
            dma((groups,)),
            dma(()),
            dma(()),
            dma(()),
            dma(()),
            dma(()),
            dma(()),
        ],
        compiler_params=pltpu.CompilerParams(collective_id=0, has_side_effects=True),
    )(signal, cotangent, long_filter, *[jnp.asarray(table) for table in tables])
    gs_rows, gf_rows = (
        pltpu.with_memory_space_constraint(rows, pltpu.VMEM) for rows in (gs_rows, gf_rows)
    )
    result = jax.ShapeDtypeStruct((positions, columns), bf16)
    return pl.pallas_call(
        functools.partial(place_columns, columns // LANES),
        name="place_columns",
        out_shape=(result, result),
        in_specs=[whole] * 2,
        out_specs=(whole, whole),
    )(gs_rows, gf_rows)


def solution(mesh):
    in_specs = (P("cp", "tp"), P("cp", "tp"), P("cp", None))
    out_specs = (P("cp", "tp"), P("cp", None))
    run = functools.partial(body, mesh.shape["tp"], mesh.shape["cp"])
    return jax.shard_map(run, mesh=mesh, in_specs=in_specs, out_specs=out_specs, check_vma=False)
```

```python
import functools

import jax
import jax.numpy as jnp
import ml_dtypes
import numpy as np
from jax import lax
from jax.experimental import pallas as pl
from jax.experimental.pallas import tpu as pltpu
from jax.sharding import PartitionSpec as P

MESH = pl.DeviceIdType.MESH
bf16, f32 = jnp.bfloat16, jnp.float32
LANES = 128


def split_np(table):
    high = table.astype(ml_dtypes.bfloat16)
    low = (table - high.astype(np.float64)).astype(ml_dtypes.bfloat16)
    return high, low


def make_tables(blocks):
    half = 2 * blocks
    total = half * LANES
    w = np.arange(blocks) + 0.5
    k = np.arange(blocks)
    angle = 2 * np.pi * np.outer(w, k) / half
    pair = np.eye(2)
    cos_wk, sin_wk = np.kron(np.cos(angle), pair), np.kron(np.sin(angle), pair)
    filt = np.concatenate([cos_wk, -sin_wk], axis=0)
    both = np.zeros((2, 2, blocks, 2, blocks, 2, 2))
    for a in range(2):
        for c in range(2):
            both[a, 0, :, c, :, a, c] = np.cos(angle)
            both[a, 1, :, c, :, a, c] = -np.sin(angle)
    both = both.reshape(8 * blocks, 4 * blocks)
    lane = np.arange(LANES)
    twist = 2 * np.pi * np.outer(np.repeat(w, 2), lane) / total
    turn = 2 * np.pi * np.outer(lane, lane) / LANES
    cos_t, sin_t = np.cos(turn), np.sin(turn)
    forward = np.block([[cos_t, -sin_t], [sin_t, cos_t]])
    back = np.concatenate([cos_wk.T, -sin_wk.T], axis=1) * (2.0 / total)
    both_h, both_l = split_np(both)
    filt_h, filt_l = split_np(filt)
    forw_h, forw_l = split_np(forward)
    inv_h, inv_l = split_np(forward.T)
    back_h, back_l = split_np(back)
    tables = (
        np.concatenate([both_h, both_l], axis=1),
        np.concatenate([filt_h, filt_l], axis=1),
        np.stack([np.cos(twist), np.sin(twist)]).astype(np.float32),
        np.stack([forw_h, forw_l]),
        np.stack([inv_h, inv_l]),
        np.concatenate([back_h, back_h, back_l], axis=1),
    )
    return tables


def permutation(groups):
    table = np.zeros((groups, 2, 2, 2, groups, 2), np.float32)
    for d in range(groups):
        for a in range(2):
            for c in range(2):
                table[d, a, c, a, d, c] = 1
    return table.reshape(4 * groups, 4 * groups)


def dot(left, right):
    return lax.dot_general(left, right, (((1,), (0,)), ((), ())), preferred_element_type=f32)


def dot_nt(left, right):
    return lax.dot_general(left, right, (((1,), (1,)), ((), ())), preferred_element_type=f32)


def split(value):
    high = value.astype(bf16)
    low = (value - high.astype(f32)).astype(bf16)
    return high, low


def dot3(value, table_ref):
    high, low = split(value)
    top, bottom = table_ref[0], table_ref[1]
    return dot(high, top) + (dot(low, top) + dot(high, bottom))


def far_first(size):
    return sorted(range(size), key=lambda o: -min(o, size - o))


def exchange(groups, blocks, sig_hbm, cot_hbm, fil_hbm, *refs):
    tables_hbm, rest = refs[:7], refs[7:]
    out_gs, out_gf = rest[:2]
    sig, cot, fil = rest[2:5]
    both, filt, twist, forw, inv, back, perm = rest[5:12]
    (send, send_f, recv, recv_f, ready, ready_f) = rest[12:18]
    (load_sem, send_sem, recv_sem, send_f_sem, recv_f_sem) = rest[18:23]
    (gs_out_sem, gs_in_sem, gf_out_sem, gf_in_sem) = rest[23:]
    t = lax.axis_index("tp")
    p = lax.axis_index("cp")
    me = t * blocks + p
    devices = groups * blocks
    xs, lows = groups // 2, blocks // 8
    x, high = t // 2, lax.rem(t, 2)
    z, rest_p = high * lows + p // 8, lax.rem(p, 8)

    def greet_all(loads):
        barrier = pltpu.get_barrier_semaphore()
        for z_off in far_first(2 * lows):
            if z_off == lows - 2:
                for load in loads:
                    load.start()
            z_to = lax.rem(z + z_off, 2 * lows)
            for x_off in far_first(xs):
                group = lax.rem(x + x_off, xs) * 2 + z_to // lows
                base = lax.rem(z_to, lows) * 8

                def greet(i, _, group=group, base=base):
                    place = base + lax.rem(rest_p + i, 8)
                    pl.semaphore_signal(
                        barrier, inc=1, device_id=(group, place), device_id_type=MESH
                    )
                    return 0

                lax.fori_loop(
                    1 if z_off == 0 and x_off == 0 else 0, 8, greet, 0, unroll=True
                )

    steps = [(x_off, h_off) for x_off in far_first(xs) for h_off in (1, 0)]
    steps = sorted(steps, key=lambda o: -min(o[0], xs - o[0]) - 0.5 * o[1])
    sizes = (groups // 4, groups // 4, groups // 2)

    def there(step):
        return lax.rem(x + step[0], xs) * 2 + lax.rem(high + step[1], 2)

    def origin(step):
        return lax.rem(x + xs - step[0], xs) * 2 + lax.rem(high + step[1], 2)

    def places(step, act):
        def one(i, _):
            act(lax.rem(p + i, blocks))
            return 0

        lax.fori_loop(1 if step == (0, 0) else 0, blocks, one, 0, unroll=8)

    loads = [
        pltpu.make_async_copy(source, target, load_sem.at[i])
        for i, (source, target) in enumerate(
            zip(
                (sig_hbm, cot_hbm, fil_hbm) + tuple(tables_hbm),
                (sig, cot, fil, both, filt, twist, forw, inv, back, perm),
                strict=True,
            )
        )
    ]
    greet_all(loads)
    for load in loads:
        load.wait()

    eye = identity()
    per = LANES // 2
    for q in range(2 * devices // LANES):
        cols = pl.ds(q * LANES, LANES)
        pair = jnp.concatenate([sig[:, cols], cot[:, cols]], axis=1)
        moved = dot_nt(perm[...], pair)
        send[pl.ds(q * per, per)] = moved.reshape(per, 4, LANES).astype(bf16)
        moved = dot_nt(eye, fil[:, cols])
        send_f[pl.ds(q * per, per)] = moved.reshape(per, 2, LANES).astype(bf16)

    pl.semaphore_wait(pltpu.get_barrier_semaphore(), devices - 1)

    pltpu.make_async_copy(send_f.at[me], recv_f.at[p], recv_f_sem).start()

    def give_filter(place):
        pltpu.make_async_remote_copy(
            send_f.at[t * blocks + place],
            recv_f.at[p],
            send_f_sem,
            recv_f_sem,
            device_id=(t, place),
            device_id_type=MESH,
        ).start()

    for n, step in enumerate(steps):
        if n == len(steps) // 4:
            places((0, 0), give_filter)
        group = there(step)

        def give(place, n=n, group=group):
            pltpu.make_async_remote_copy(
                send.at[group * blocks + place],
                recv.at[me],
                send_sem,
                recv_sem.at[n],
                device_id=(group, place),
                device_id_type=MESH,
            ).start()

        places(step, give)
        if tuple(step) == (0, 0):
            pltpu.make_async_copy(send.at[me], recv.at[me], recv_sem.at[n]).start()

    turn_c, turn_s = twist[0], twist[1]
    width = 2 * blocks

    def turn(real, imag):
        return jnp.concatenate(
            [real * turn_c + imag * turn_s, imag * turn_c - real * turn_s], axis=1
        )

    def unturn(part):
        g_real, g_imag = part[:, :LANES], part[:, LANES:]
        return jnp.concatenate(
            [g_real * turn_c - g_imag * turn_s, g_real * turn_s + g_imag * turn_c], axis=0
        )

    def inverse(spectra):
        part = dot3(
            jnp.concatenate([jnp.concatenate(pair, axis=1) for pair in spectra], axis=0), inv
        )
        turned = [unturn(part[i * width : (i + 1) * width]) for i in range(len(spectra))]
        results = []
        for i in range(0, len(turned), 2):
            some = turned[i : i + 2]
            high_part, low_part = split(jnp.concatenate(some, axis=1))
            rows = dot(back[...], jnp.concatenate([high_part, low_part, high_part], axis=0))
            for n in range(len(some)):
                result = rows[:, n * LANES : (n + 1) * LANES]
                results.append(result.reshape(blocks, 2, LANES).astype(bf16))
        return results

    head = 1
    turn_to_head = lax.rem(head - p + blocks, blocks)

    def all_but_head(group, act):
        def one(i, _):
            act(lax.rem(p + i, blocks))
            return 0

        @pl.when(group == 0)
        def _():
            @pl.when(jnp.logical_and(t != 0, p != head))
            def _():
                act(p)

            lax.fori_loop(1, turn_to_head, one, 0)
            lax.fori_loop(turn_to_head + 1, blocks, one, 0)

        @pl.when(group != 0)
        def _():
            @pl.when(group != t)
            def _():
                act(p)

            lax.fori_loop(1, blocks, one, 0, unroll=8)

    def give_row(group, place):
        pltpu.make_async_remote_copy(
            ready.at[group * blocks + place],
            out_gs.at[me],
            gs_out_sem,
            gs_in_sem,
            device_id=(group, place),
            device_id_type=MESH,
        ).start()

    def give_rows(step, late):
        group = origin(step)
        if late:
            all_but_head(group, functools.partial(give_row, group))
        else:
            places(step, functools.partial(give_row, group))
        if step == (0, 0):
            pltpu.make_async_copy(ready.at[me], out_gs.at[me], gs_in_sem).start()

    def give_sum(group, place):
        pltpu.make_async_remote_copy(
            ready_f.at[place],
            out_gf.at[me],
            gf_out_sem,
            gf_in_sem,
            device_id=(group, place),
            device_id_type=MESH,
        ).start()

    def give_sums(half):
        for x_off in far_first(xs):
            group = lax.rem(x + xs - x_off, xs) * 2 + half
            all_but_head(group, functools.partial(give_sum, group))

    pltpu.make_async_copy(recv_f, recv_f, recv_f_sem).wait()
    data = recv_f[...].reshape(2 * blocks, LANES)
    halves = dot(filt[...], jnp.concatenate([data, data], axis=0))
    h_spec = dot3(turn(halves[:width], halves[width:]), forw)
    h_real, h_imag = h_spec[:, :LANES], h_spec[:, LANES:]

    sum_real = jnp.zeros((width, LANES), f32)
    sum_imag = jnp.zeros((width, LANES), f32)
    first = 0
    for size in sizes:
        some = range(first, first + size)
        first += size
        mine = [pl.ds(origin(steps[n]) * blocks, blocks) for n in some]
        for n, rows in zip(some, mine, strict=True):
            pltpu.make_async_copy(recv.at[rows], recv.at[rows], recv_sem.at[n]).wait()
        turned = []
        for i in range(0, size, 2):
            data = jnp.concatenate(
                [recv[rows].reshape(4 * blocks, LANES) for rows in mine[i : i + 2]], axis=1
            )
            halves = dot(both[...], jnp.concatenate([data, data], axis=0))
            for n in range(len(mine[i : i + 2])):
                part = halves[:, n * LANES : (n + 1) * LANES]
                turned.append(turn(part[:width], part[width : 2 * width]))
                turned.append(turn(part[2 * width : 3 * width], part[3 * width :]))
        spec = dot3(jnp.concatenate(turned, axis=0), forw)
        products = []
        for n in range(size):
            u_spec = spec[2 * n * width : (2 * n + 1) * width]
            d_spec = spec[(2 * n + 1) * width : (2 * n + 2) * width]
            u_real, u_imag = u_spec[:, :LANES], u_spec[:, LANES:]
            d_real, d_imag = d_spec[:, :LANES], d_spec[:, LANES:]
            sum_real = sum_real + (u_real * d_real + u_imag * d_imag)
            sum_imag = sum_imag + (u_real * d_imag - u_imag * d_real)
            products.append(
                (h_real * d_real + h_imag * d_imag, h_real * d_imag - h_imag * d_real)
            )
        if first == len(steps):
            products.append((sum_real, sum_imag))
        results = inverse(products)
        late = first == len(steps)
        if late:
            ready_f[...] = results[-1]
        for rows, result in zip(mine, results[:size], strict=True):
            ready[rows] = result
        if late:
            pltpu.make_async_copy(ready_f.at[p], out_gf.at[me], gf_in_sem).start()

            @pl.when(me != head)
            def _():
                give_sum(0, head)

            for n in some:

                @pl.when(jnp.logical_and(origin(steps[n]) == 0, me != head))
                def _():
                    give_row(0, head)

            give_sums(0)
        for n in sorted(some, key=lambda n: -steps[n][1]):
            give_rows(steps[n], late)
    give_sums(1)

    some = pl.ds(0, devices - 1)
    pltpu.make_async_copy(send.at[some], send.at[some], send_sem).wait()
    pltpu.make_async_copy(ready.at[some], ready.at[some], gs_out_sem).wait()
    few = pl.ds(0, blocks - 1)
    pltpu.make_async_copy(send_f.at[few], send_f.at[few], send_f_sem).wait()
    pltpu.make_async_copy(out_gf.at[some], out_gf.at[some], gf_out_sem).wait()
    pltpu.make_async_copy(out_gs, out_gs, gs_in_sem).wait()
    pltpu.make_async_copy(out_gf, out_gf, gf_in_sem).wait()


def identity():
    rows = lax.broadcasted_iota(jnp.int32, (LANES, LANES), 0)
    cols = lax.broadcasted_iota(jnp.int32, (LANES, LANES), 1)
    return (rows == cols).astype(f32).astype(bf16)


def place_columns(quarters, gs_in, gf_in, gs_ref, gf_ref):
    eye = identity()
    per = LANES // 2
    for q in range(quarters):
        for source, target in ((gs_in, gs_ref), (gf_in, gf_ref)):
            block = source[pl.ds(q * per, per)].reshape(LANES, LANES)
            target[:, pl.ds(q * LANES, LANES)] = dot_nt(eye, block).astype(bf16)


def body(groups, blocks, signal, cotangent, long_filter):
    positions, columns = signal.shape
    devices = groups * blocks
    tables = make_tables(blocks) + (permutation(LANES // 2).astype(ml_dtypes.bfloat16),)
    vmem = pltpu.VMEM
    dma = pltpu.SemaphoreType.DMA
    anywhere = pl.BlockSpec(memory_space=pl.ANY)
    whole = pl.BlockSpec(memory_space=pltpu.VMEM)
    pairs = pltpu.VMEM((devices, 2, LANES), bf16)
    gs_rows, gf_rows = pl.pallas_call(
        functools.partial(exchange, groups, blocks),
        name="exchange",
        out_shape=(pairs, pairs),
        in_specs=[anywhere] * (3 + len(tables)),
        out_specs=(whole, whole),
        scratch_shapes=[vmem((positions, columns), bf16)] * 3
        + [vmem(table.shape, table.dtype) for table in tables]
        + [
            vmem((devices, 4, LANES), bf16),
            vmem((devices, 2, LANES), bf16),
            vmem((devices, 4, LANES), bf16),
            vmem((blocks, 2, LANES), bf16),
            vmem((devices, 2, LANES), bf16),
            vmem((blocks, 2, LANES), bf16),
            dma((3 + len(tables),)),
            dma(()),
            dma((groups,)),
            dma(()),
            dma(()),
            dma(()),
            dma(()),
            dma(()),
            dma(()),
        ],
        compiler_params=pltpu.CompilerParams(collective_id=0, has_side_effects=True),
    )(signal, cotangent, long_filter, *[jnp.asarray(table) for table in tables])
    gs_rows, gf_rows = (
        pltpu.with_memory_space_constraint(rows, pltpu.VMEM) for rows in (gs_rows, gf_rows)
    )
    result = jax.ShapeDtypeStruct((positions, columns), bf16)
    return pl.pallas_call(
        functools.partial(place_columns, columns // LANES),
        name="place_columns",
        out_shape=(result, result),
        in_specs=[whole] * 2,
        out_specs=(whole, whole),
    )(gs_rows, gf_rows)


def solution(mesh):
    in_specs = (P("cp", "tp"), P("cp", "tp"), P("cp", None))
    out_specs = (P("cp", "tp"), P("cp", None))
    run = functools.partial(body, mesh.shape["tp"], mesh.shape["cp"])
    return jax.shard_map(run, mesh=mesh, in_specs=in_specs, out_specs=out_specs, check_vma=False)
```

```python
import functools

import jax
import jax.numpy as jnp
import ml_dtypes
import numpy as np
from jax import lax
from jax.experimental import pallas as pl
from jax.experimental.pallas import tpu as pltpu
from jax.sharding import PartitionSpec as P

MESH = pl.DeviceIdType.MESH
bf16, f32 = jnp.bfloat16, jnp.float32
LANES = 128


def split_np(table):
    high = table.astype(ml_dtypes.bfloat16)
    low = (table - high.astype(np.float64)).astype(ml_dtypes.bfloat16)
    return high, low


def make_tables(blocks):
    half = 2 * blocks
    total = half * LANES
    w = np.arange(blocks) + 0.5
    k = np.arange(blocks)
    angle = 2 * np.pi * np.outer(w, k) / half
    pair = np.eye(2)
    cos_wk, sin_wk = np.kron(np.cos(angle), pair), np.kron(np.sin(angle), pair)
    filt = np.concatenate([cos_wk, -sin_wk], axis=0)
    both = np.zeros((2, 2, blocks, 2, blocks, 2, 2))
    for a in range(2):
        for c in range(2):
            both[a, 0, :, c, :, a, c] = np.cos(angle)
            both[a, 1, :, c, :, a, c] = -np.sin(angle)
    both = both.reshape(8 * blocks, 4 * blocks)
    lane = np.arange(LANES)
    twist = 2 * np.pi * np.outer(np.repeat(w, 2), lane) / total
    turn = 2 * np.pi * np.outer(lane, lane) / LANES
    cos_t, sin_t = np.cos(turn), np.sin(turn)
    forward = np.block([[cos_t, -sin_t], [sin_t, cos_t]])
    back = np.concatenate([cos_wk.T, -sin_wk.T], axis=1) * (2.0 / total)
    both_h, both_l = split_np(both)
    filt_h, filt_l = split_np(filt)
    forw_h, forw_l = split_np(forward)
    inv_h, inv_l = split_np(forward.T)
    back_h, back_l = split_np(back)
    tables = (
        np.concatenate([both_h, both_l], axis=1),
        np.concatenate([filt_h, filt_l], axis=1),
        np.stack([np.cos(twist), np.sin(twist)]).astype(np.float32),
        np.stack([forw_h, forw_l]),
        np.stack([inv_h, inv_l]),
        np.concatenate([back_h, back_h, back_l], axis=1),
    )
    return tables


def permutation(groups):
    table = np.zeros((groups, 2, 2, 2, groups, 2), np.float32)
    for d in range(groups):
        for a in range(2):
            for c in range(2):
                table[d, a, c, a, d, c] = 1
    return table.reshape(4 * groups, 4 * groups)


def dot(left, right):
    return lax.dot_general(left, right, (((1,), (0,)), ((), ())), preferred_element_type=f32)


def dot_nt(left, right):
    return lax.dot_general(left, right, (((1,), (1,)), ((), ())), preferred_element_type=f32)


def split(value):
    high = value.astype(bf16)
    low = (value - high.astype(f32)).astype(bf16)
    return high, low


def dot3(value, table_ref):
    high, low = split(value)
    top, bottom = table_ref[0], table_ref[1]
    return dot(high, top) + (dot(low, top) + dot(high, bottom))


def far_first(size):
    return sorted(range(size), key=lambda o: -min(o, size - o))


def exchange(groups, blocks, sig_hbm, cot_hbm, fil_hbm, *refs):
    tables_hbm, rest = refs[:7], refs[7:]
    out_gs, out_gf = rest[:2]
    sig, cot, fil = rest[2:5]
    both, filt, twist, forw, inv, back, perm = rest[5:12]
    (send, send_f, recv, recv_f, ready, ready_f) = rest[12:18]
    (load_sem, send_sem, recv_sem, send_f_sem, recv_f_sem) = rest[18:23]
    (gs_out_sem, gs_in_sem, gf_out_sem, gf_in_sem) = rest[23:]
    t = lax.axis_index("tp")
    p = lax.axis_index("cp")
    me = t * blocks + p
    devices = groups * blocks
    xs, lows = groups // 2, blocks // 8
    x, high = t // 2, lax.rem(t, 2)
    z, rest_p = high * lows + p // 8, lax.rem(p, 8)

    def greet_all(loads):
        barrier = pltpu.get_barrier_semaphore()
        for z_off in far_first(2 * lows):
            if z_off == 0:
                for load in loads:
                    load.start()
            z_to = lax.rem(z + z_off, 2 * lows)
            for x_off in far_first(xs):
                group = lax.rem(x + x_off, xs) * 2 + z_to // lows
                base = lax.rem(z_to, lows) * 8

                def greet(i, _, group=group, base=base):
                    place = base + lax.rem(rest_p + i, 8)
                    pl.semaphore_signal(
                        barrier, inc=1, device_id=(group, place), device_id_type=MESH
                    )
                    return 0

                lax.fori_loop(
                    1 if z_off == 0 and x_off == 0 else 0, 8, greet, 0, unroll=True
                )

    steps = [(x_off, h_off) for x_off in far_first(xs) for h_off in (1, 0)]
    steps = sorted(steps, key=lambda o: -min(o[0], xs - o[0]) - 0.5 * o[1])
    sizes = (groups // 4, groups // 4, groups // 2)

    def there(step):
        return lax.rem(x + step[0], xs) * 2 + lax.rem(high + step[1], 2)

    def origin(step):
        return lax.rem(x + xs - step[0], xs) * 2 + lax.rem(high + step[1], 2)

    def places(step, act):
        def one(i, _):
            act(lax.rem(p + i, blocks))
            return 0

        lax.fori_loop(1 if step == (0, 0) else 0, blocks, one, 0, unroll=8)

    loads = [
        pltpu.make_async_copy(source, target, load_sem.at[i])
        for i, (source, target) in enumerate(
            zip(
                (sig_hbm, cot_hbm, fil_hbm) + tuple(tables_hbm),
                (sig, cot, fil, both, filt, twist, forw, inv, back, perm),
                strict=True,
            )
        )
    ]
    greet_all(loads)
    for load in loads:
        load.wait()

    eye = identity()
    per = LANES // 2
    for q in range(2 * devices // LANES):
        cols = pl.ds(q * LANES, LANES)
        pair = jnp.concatenate([sig[:, cols], cot[:, cols]], axis=1)
        moved = dot_nt(perm[...], pair)
        send[pl.ds(q * per, per)] = moved.reshape(per, 4, LANES).astype(bf16)
        moved = dot_nt(eye, fil[:, cols])
        send_f[pl.ds(q * per, per)] = moved.reshape(per, 2, LANES).astype(bf16)

    pl.semaphore_wait(pltpu.get_barrier_semaphore(), devices - 1)

    pltpu.make_async_copy(send_f.at[me], recv_f.at[p], recv_f_sem).start()

    def give_filter(place):
        pltpu.make_async_remote_copy(
            send_f.at[t * blocks + place],
            recv_f.at[p],
            send_f_sem,
            recv_f_sem,
            device_id=(t, place),
            device_id_type=MESH,
        ).start()

    for n, step in enumerate(steps):
        if n == len(steps) // 4:
            places((0, 0), give_filter)
        group = there(step)

        def give(place, n=n, group=group):
            pltpu.make_async_remote_copy(
                send.at[group * blocks + place],
                recv.at[me],
                send_sem,
                recv_sem.at[n],
                device_id=(group, place),
                device_id_type=MESH,
            ).start()

        places(step, give)
        if tuple(step) == (0, 0):
            pltpu.make_async_copy(send.at[me], recv.at[me], recv_sem.at[n]).start()

    turn_c, turn_s = twist[0], twist[1]
    width = 2 * blocks

    def turn(real, imag):
        return jnp.concatenate(
            [real * turn_c + imag * turn_s, imag * turn_c - real * turn_s], axis=1
        )

    def unturn(part):
        g_real, g_imag = part[:, :LANES], part[:, LANES:]
        return jnp.concatenate(
            [g_real * turn_c - g_imag * turn_s, g_real * turn_s + g_imag * turn_c], axis=0
        )

    def inverse(spectra):
        part = dot3(
            jnp.concatenate([jnp.concatenate(pair, axis=1) for pair in spectra], axis=0), inv
        )
        turned = [unturn(part[i * width : (i + 1) * width]) for i in range(len(spectra))]
        results = []
        for i in range(0, len(turned), 2):
            some = turned[i : i + 2]
            high_part, low_part = split(jnp.concatenate(some, axis=1))
            rows = dot(back[...], jnp.concatenate([high_part, low_part, high_part], axis=0))
            for n in range(len(some)):
                result = rows[:, n * LANES : (n + 1) * LANES]
                results.append(result.reshape(blocks, 2, LANES).astype(bf16))
        return results

    head = 1
    turn_to_head = lax.rem(head - p + blocks, blocks)

    def all_but_head(group, act):
        def one(i, _):
            act(lax.rem(p + i, blocks))
            return 0

        @pl.when(group == 0)
        def _():
            @pl.when(jnp.logical_and(t != 0, p != head))
            def _():
                act(p)

            lax.fori_loop(1, turn_to_head, one, 0)
            lax.fori_loop(turn_to_head + 1, blocks, one, 0)

        @pl.when(group != 0)
        def _():
            @pl.when(group != t)
            def _():
                act(p)

            lax.fori_loop(1, blocks, one, 0, unroll=8)

    def give_row(group, place):
        pltpu.make_async_remote_copy(
            ready.at[group * blocks + place],
            out_gs.at[me],
            gs_out_sem,
            gs_in_sem,
            device_id=(group, place),
            device_id_type=MESH,
        ).start()

    def give_rows(step, late):
        group = origin(step)
        if late:
            all_but_head(group, functools.partial(give_row, group))
        else:
            places(step, functools.partial(give_row, group))
        if step == (0, 0):
            pltpu.make_async_copy(ready.at[me], out_gs.at[me], gs_in_sem).start()

    def give_sum(group, place):
        pltpu.make_async_remote_copy(
            ready_f.at[place],
            out_gf.at[me],
            gf_out_sem,
            gf_in_sem,
            device_id=(group, place),
            device_id_type=MESH,
        ).start()

    def give_sums(half):
        for x_off in far_first(xs):
            group = lax.rem(x + xs - x_off, xs) * 2 + half
            all_but_head(group, functools.partial(give_sum, group))

    pltpu.make_async_copy(recv_f, recv_f, recv_f_sem).wait()
    data = recv_f[...].reshape(2 * blocks, LANES)
    halves = dot(filt[...], jnp.concatenate([data, data], axis=0))
    h_spec = dot3(turn(halves[:width], halves[width:]), forw)
    h_real, h_imag = h_spec[:, :LANES], h_spec[:, LANES:]

    sum_real = jnp.zeros((width, LANES), f32)
    sum_imag = jnp.zeros((width, LANES), f32)
    first = 0
    for size in sizes:
        some = range(first, first + size)
        first += size
        mine = [pl.ds(origin(steps[n]) * blocks, blocks) for n in some]
        for n, rows in zip(some, mine, strict=True):
            pltpu.make_async_copy(recv.at[rows], recv.at[rows], recv_sem.at[n]).wait()
        turned = []
        for i in range(0, size, 2):
            data = jnp.concatenate(
                [recv[rows].reshape(4 * blocks, LANES) for rows in mine[i : i + 2]], axis=1
            )
            halves = dot(both[...], jnp.concatenate([data, data], axis=0))
            for n in range(len(mine[i : i + 2])):
                part = halves[:, n * LANES : (n + 1) * LANES]
                turned.append(turn(part[:width], part[width : 2 * width]))
                turned.append(turn(part[2 * width : 3 * width], part[3 * width :]))
        spec = dot3(jnp.concatenate(turned, axis=0), forw)
        products = []
        for n in range(size):
            u_spec = spec[2 * n * width : (2 * n + 1) * width]
            d_spec = spec[(2 * n + 1) * width : (2 * n + 2) * width]
            u_real, u_imag = u_spec[:, :LANES], u_spec[:, LANES:]
            d_real, d_imag = d_spec[:, :LANES], d_spec[:, LANES:]
            sum_real = sum_real + (u_real * d_real + u_imag * d_imag)
            sum_imag = sum_imag + (u_real * d_imag - u_imag * d_real)
            products.append(
                (h_real * d_real + h_imag * d_imag, h_real * d_imag - h_imag * d_real)
            )
        if first == len(steps):
            products.append((sum_real, sum_imag))
        results = inverse(products)
        late = first == len(steps)
        if late:
            ready_f[...] = results[-1]
        for rows, result in zip(mine, results[:size], strict=True):
            ready[rows] = result
        if late:
            pltpu.make_async_copy(ready_f.at[p], out_gf.at[me], gf_in_sem).start()

            @pl.when(me != head)
            def _():
                give_sum(0, head)

            for n in some:

                @pl.when(jnp.logical_and(origin(steps[n]) == 0, me != head))
                def _():
                    give_row(0, head)

            give_sums(0)
        for n in sorted(some, key=lambda n: -steps[n][1]):
            give_rows(steps[n], late)
    give_sums(1)

    some = pl.ds(0, devices - 1)
    pltpu.make_async_copy(send.at[some], send.at[some], send_sem).wait()
    pltpu.make_async_copy(ready.at[some], ready.at[some], gs_out_sem).wait()
    few = pl.ds(0, blocks - 1)
    pltpu.make_async_copy(send_f.at[few], send_f.at[few], send_f_sem).wait()
    pltpu.make_async_copy(out_gf.at[some], out_gf.at[some], gf_out_sem).wait()
    pltpu.make_async_copy(out_gs, out_gs, gs_in_sem).wait()
    pltpu.make_async_copy(out_gf, out_gf, gf_in_sem).wait()


def identity():
    rows = lax.broadcasted_iota(jnp.int32, (LANES, LANES), 0)
    cols = lax.broadcasted_iota(jnp.int32, (LANES, LANES), 1)
    return (rows == cols).astype(f32).astype(bf16)


def place_columns(quarters, gs_in, gf_in, gs_ref, gf_ref):
    eye = identity()
    per = LANES // 2
    for q in range(quarters):
        for source, target in ((gs_in, gs_ref), (gf_in, gf_ref)):
            block = source[pl.ds(q * per, per)].reshape(LANES, LANES)
            target[:, pl.ds(q * LANES, LANES)] = dot_nt(eye, block).astype(bf16)


def body(groups, blocks, signal, cotangent, long_filter):
    positions, columns = signal.shape
    devices = groups * blocks
    tables = make_tables(blocks) + (permutation(LANES // 2).astype(ml_dtypes.bfloat16),)
    vmem = pltpu.VMEM
    dma = pltpu.SemaphoreType.DMA
    anywhere = pl.BlockSpec(memory_space=pl.ANY)
    whole = pl.BlockSpec(memory_space=pltpu.VMEM)
    pairs = pltpu.VMEM((devices, 2, LANES), bf16)
    gs_rows, gf_rows = pl.pallas_call(
        functools.partial(exchange, groups, blocks),
        name="exchange",
        out_shape=(pairs, pairs),
        in_specs=[anywhere] * (3 + len(tables)),
        out_specs=(whole, whole),
        scratch_shapes=[vmem((positions, columns), bf16)] * 3
        + [vmem(table.shape, table.dtype) for table in tables]
        + [
            vmem((devices, 4, LANES), bf16),
            vmem((devices, 2, LANES), bf16),
            vmem((devices, 4, LANES), bf16),
            vmem((blocks, 2, LANES), bf16),
            vmem((devices, 2, LANES), bf16),
            vmem((blocks, 2, LANES), bf16),
            dma((3 + len(tables),)),
            dma(()),
            dma((groups,)),
            dma(()),
            dma(()),
            dma(()),
            dma(()),
            dma(()),
            dma(()),
        ],
        compiler_params=pltpu.CompilerParams(collective_id=0, has_side_effects=True),
    )(signal, cotangent, long_filter, *[jnp.asarray(table) for table in tables])
    gs_rows, gf_rows = (
        pltpu.with_memory_space_constraint(rows, pltpu.VMEM) for rows in (gs_rows, gf_rows)
    )
    result = jax.ShapeDtypeStruct((positions, columns), bf16)
    return pl.pallas_call(
        functools.partial(place_columns, columns // LANES),
        name="place_columns",
        out_shape=(result, result),
        in_specs=[whole] * 2,
        out_specs=(whole, whole),
    )(gs_rows, gf_rows)


def solution(mesh):
    in_specs = (P("cp", "tp"), P("cp", "tp"), P("cp", None))
    out_specs = (P("cp", "tp"), P("cp", None))
    run = functools.partial(body, mesh.shape["tp"], mesh.shape["cp"])
    return jax.shard_map(run, mesh=mesh, in_specs=in_specs, out_specs=out_specs, check_vma=False)
```

```python
import functools

import jax
import jax.numpy as jnp
import ml_dtypes
import numpy as np
from jax import lax
from jax.experimental import pallas as pl
from jax.experimental.pallas import tpu as pltpu
from jax.sharding import PartitionSpec as P

MESH = pl.DeviceIdType.MESH
bf16, f32 = jnp.bfloat16, jnp.float32
LANES = 128


def split_np(table):
    high = table.astype(ml_dtypes.bfloat16)
    low = (table - high.astype(np.float64)).astype(ml_dtypes.bfloat16)
    return high, low


def make_tables(blocks):
    half = 2 * blocks
    total = half * LANES
    w = np.arange(blocks) + 0.5
    k = np.arange(blocks)
    angle = 2 * np.pi * np.outer(w, k) / half
    pair = np.eye(2)
    cos_wk, sin_wk = np.kron(np.cos(angle), pair), np.kron(np.sin(angle), pair)
    filt = np.concatenate([cos_wk, -sin_wk], axis=0)
    both = np.zeros((2, 2, blocks, 2, blocks, 2, 2))
    for a in range(2):
        for c in range(2):
            both[a, 0, :, c, :, a, c] = np.cos(angle)
            both[a, 1, :, c, :, a, c] = -np.sin(angle)
    both = both.reshape(8 * blocks, 4 * blocks)
    lane = np.arange(LANES)
    twist = 2 * np.pi * np.outer(np.repeat(w, 2), lane) / total
    turn = 2 * np.pi * np.outer(lane, lane) / LANES
    cos_t, sin_t = np.cos(turn), np.sin(turn)
    forward = np.block([[cos_t, -sin_t], [sin_t, cos_t]])
    back = np.concatenate([cos_wk.T, -sin_wk.T], axis=1) * (2.0 / total)
    both_h, both_l = split_np(both)
    filt_h, filt_l = split_np(filt)
    forw_h, forw_l = split_np(forward)
    inv_h, inv_l = split_np(forward.T)
    back_h, back_l = split_np(back)
    tables = (
        np.concatenate([both_h, both_l], axis=1),
        np.concatenate([filt_h, filt_l], axis=1),
        np.stack([np.cos(twist), np.sin(twist)]).astype(np.float32),
        np.stack([forw_h, forw_l]),
        np.stack([inv_h, inv_l]),
        np.concatenate([back_h, back_h, back_l], axis=1),
    )
    return tables


def permutation(groups):
    table = np.zeros((groups, 2, 2, 2, groups, 2), np.float32)
    for d in range(groups):
        for a in range(2):
            for c in range(2):
                table[d, a, c, a, d, c] = 1
    return table.reshape(4 * groups, 4 * groups)


def dot(left, right):
    return lax.dot_general(left, right, (((1,), (0,)), ((), ())), preferred_element_type=f32)


def dot_nt(left, right):
    return lax.dot_general(left, right, (((1,), (1,)), ((), ())), preferred_element_type=f32)


def split(value):
    high = value.astype(bf16)
    low = (value - high.astype(f32)).astype(bf16)
    return high, low


def dot3(value, table_ref):
    high, low = split(value)
    top, bottom = table_ref[0], table_ref[1]
    return dot(high, top) + (dot(low, top) + dot(high, bottom))


def far_first(size):
    return sorted(range(size), key=lambda o: -min(o, size - o))


def exchange(groups, blocks, sig_hbm, cot_hbm, fil_hbm, *refs):
    tables_hbm, rest = refs[:7], refs[7:]
    out_gs, out_gf = rest[:2]
    sig, cot, fil = rest[2:5]
    both, filt, twist, forw, inv, back, perm = rest[5:12]
    (send, send_f, recv, recv_f, ready, ready_f) = rest[12:18]
    (load_sem, send_sem, recv_sem, send_f_sem, recv_f_sem) = rest[18:23]
    (gs_out_sem, gs_in_sem, gf_out_sem, gf_in_sem) = rest[23:]
    t = lax.axis_index("tp")
    p = lax.axis_index("cp")
    me = t * blocks + p
    devices = groups * blocks
    xs, lows = groups // 2, blocks // 8
    x, high = t // 2, lax.rem(t, 2)
    z, rest_p = high * lows + p // 8, lax.rem(p, 8)

    def greet_all(loads):
        barrier = pltpu.get_barrier_semaphore()
        for z_off in far_first(2 * lows):
            if z_off == 0:
                for load in loads:
                    load.start()
            z_to = lax.rem(z + z_off, 2 * lows)
            for x_off in far_first(xs):
                group = lax.rem(x + x_off, xs) * 2 + z_to // lows
                base = lax.rem(z_to, lows) * 8

                def greet(i, _, group=group, base=base):
                    place = base + lax.rem(rest_p + i, 8)
                    pl.semaphore_signal(
                        barrier, inc=1, device_id=(group, place), device_id_type=MESH
                    )
                    return 0

                lax.fori_loop(
                    1 if z_off == 0 and x_off == 0 else 0, 8, greet, 0, unroll=True
                )

    steps = [(x_off, h_off) for x_off in far_first(xs) for h_off in (1, 0)]
    steps = sorted(steps, key=lambda o: -min(o[0], xs - o[0]) - 0.5 * o[1])
    sizes = (groups // 4, groups // 4, groups // 2)

    def there(step):
        return lax.rem(x + step[0], xs) * 2 + lax.rem(high + step[1], 2)

    def origin(step):
        return lax.rem(x + xs - step[0], xs) * 2 + lax.rem(high + step[1], 2)

    def places(step, act):
        def one(i, _):
            act(lax.rem(p + i, blocks))
            return 0

        lax.fori_loop(1 if step == (0, 0) else 0, blocks, one, 0, unroll=8)

    loads = [
        pltpu.make_async_copy(source, target, load_sem.at[i])
        for i, (source, target) in enumerate(
            zip(
                (sig_hbm, cot_hbm, fil_hbm) + tuple(tables_hbm),
                (sig, cot, fil, both, filt, twist, forw, inv, back, perm),
                strict=True,
            )
        )
    ]
    greet_all(loads)
    for load in loads:
        load.wait()

    eye = identity()
    per = LANES // 2
    for q in range(2 * devices // LANES):
        cols = pl.ds(q * LANES, LANES)
        pair = jnp.concatenate([sig[:, cols], cot[:, cols]], axis=1)
        moved = dot_nt(perm[...], pair)
        send[pl.ds(q * per, per)] = moved.reshape(per, 4, LANES).astype(bf16)
        moved = dot_nt(eye, fil[:, cols])
        send_f[pl.ds(q * per, per)] = moved.reshape(per, 2, LANES).astype(bf16)

    pl.semaphore_wait(pltpu.get_barrier_semaphore(), devices - 1)

    pltpu.make_async_copy(send_f.at[me], recv_f.at[p], recv_f_sem).start()

    def give_filter(place):
        pltpu.make_async_remote_copy(
            send_f.at[t * blocks + place],
            recv_f.at[p],
            send_f_sem,
            recv_f_sem,
            device_id=(t, place),
            device_id_type=MESH,
        ).start()

    for n, step in enumerate(steps):
        if n == 1:
            places((0, 0), give_filter)
        group = there(step)

        def give(place, n=n, group=group):
            pltpu.make_async_remote_copy(
                send.at[group * blocks + place],
                recv.at[me],
                send_sem,
                recv_sem.at[n],
                device_id=(group, place),
                device_id_type=MESH,
            ).start()

        places(step, give)
        if tuple(step) == (0, 0):
            pltpu.make_async_copy(send.at[me], recv.at[me], recv_sem.at[n]).start()

    turn_c, turn_s = twist[0], twist[1]
    width = 2 * blocks

    def turn(real, imag):
        return jnp.concatenate(
            [real * turn_c + imag * turn_s, imag * turn_c - real * turn_s], axis=1
        )

    def unturn(part):
        g_real, g_imag = part[:, :LANES], part[:, LANES:]
        return jnp.concatenate(
            [g_real * turn_c - g_imag * turn_s, g_real * turn_s + g_imag * turn_c], axis=0
        )

    def inverse(spectra):
        part = dot3(
            jnp.concatenate([jnp.concatenate(pair, axis=1) for pair in spectra], axis=0), inv
        )
        turned = [unturn(part[i * width : (i + 1) * width]) for i in range(len(spectra))]
        results = []
        for i in range(0, len(turned), 2):
            some = turned[i : i + 2]
            high_part, low_part = split(jnp.concatenate(some, axis=1))
            rows = dot(back[...], jnp.concatenate([high_part, low_part, high_part], axis=0))
            for n in range(len(some)):
                result = rows[:, n * LANES : (n + 1) * LANES]
                results.append(result.reshape(blocks, 2, LANES).astype(bf16))
        return results

    head = 1
    turn_to_head = lax.rem(head - p + blocks, blocks)

    def all_but_head(group, act):
        def one(i, _):
            act(lax.rem(p + i, blocks))
            return 0

        @pl.when(group == 0)
        def _():
            @pl.when(jnp.logical_and(t != 0, p != head))
            def _():
                act(p)

            lax.fori_loop(1, turn_to_head, one, 0)
            lax.fori_loop(turn_to_head + 1, blocks, one, 0)

        @pl.when(group != 0)
        def _():
            @pl.when(group != t)
            def _():
                act(p)

            lax.fori_loop(1, blocks, one, 0, unroll=8)

    def give_row(group, place):
        pltpu.make_async_remote_copy(
            ready.at[group * blocks + place],
            out_gs.at[me],
            gs_out_sem,
            gs_in_sem,
            device_id=(group, place),
            device_id_type=MESH,
        ).start()

    def give_rows(step, late):
        group = origin(step)
        if late:
            all_but_head(group, functools.partial(give_row, group))
        else:
            places(step, functools.partial(give_row, group))
        if step == (0, 0):
            pltpu.make_async_copy(ready.at[me], out_gs.at[me], gs_in_sem).start()

    def give_sum(group, place):
        pltpu.make_async_remote_copy(
            ready_f.at[place],
            out_gf.at[me],
            gf_out_sem,
            gf_in_sem,
            device_id=(group, place),
            device_id_type=MESH,
        ).start()

    def give_sums(half):
        for x_off in far_first(xs):
            group = lax.rem(x + xs - x_off, xs) * 2 + half
            all_but_head(group, functools.partial(give_sum, group))

    pltpu.make_async_copy(recv_f, recv_f, recv_f_sem).wait()
    data = recv_f[...].reshape(2 * blocks, LANES)
    halves = dot(filt[...], jnp.concatenate([data, data], axis=0))
    h_spec = dot3(turn(halves[:width], halves[width:]), forw)
    h_real, h_imag = h_spec[:, :LANES], h_spec[:, LANES:]

    sum_real = jnp.zeros((width, LANES), f32)
    sum_imag = jnp.zeros((width, LANES), f32)
    first = 0
    for size in sizes:
        some = range(first, first + size)
        first += size
        mine = [pl.ds(origin(steps[n]) * blocks, blocks) for n in some]
        for n, rows in zip(some, mine, strict=True):
            pltpu.make_async_copy(recv.at[rows], recv.at[rows], recv_sem.at[n]).wait()
        turned = []
        for i in range(0, size, 2):
            data = jnp.concatenate(
                [recv[rows].reshape(4 * blocks, LANES) for rows in mine[i : i + 2]], axis=1
            )
            halves = dot(both[...], jnp.concatenate([data, data], axis=0))
            for n in range(len(mine[i : i + 2])):
                part = halves[:, n * LANES : (n + 1) * LANES]
                turned.append(turn(part[:width], part[width : 2 * width]))
                turned.append(turn(part[2 * width : 3 * width], part[3 * width :]))
        spec = dot3(jnp.concatenate(turned, axis=0), forw)
        products = []
        for n in range(size):
            u_spec = spec[2 * n * width : (2 * n + 1) * width]
            d_spec = spec[(2 * n + 1) * width : (2 * n + 2) * width]
            u_real, u_imag = u_spec[:, :LANES], u_spec[:, LANES:]
            d_real, d_imag = d_spec[:, :LANES], d_spec[:, LANES:]
            sum_real = sum_real + (u_real * d_real + u_imag * d_imag)
            sum_imag = sum_imag + (u_real * d_imag - u_imag * d_real)
            products.append(
                (h_real * d_real + h_imag * d_imag, h_real * d_imag - h_imag * d_real)
            )
        if first == len(steps):
            products.append((sum_real, sum_imag))
        results = inverse(products)
        late = first == len(steps)
        if late:
            ready_f[...] = results[-1]
        for rows, result in zip(mine, results[:size], strict=True):
            ready[rows] = result
        if late:
            pltpu.make_async_copy(ready_f.at[p], out_gf.at[me], gf_in_sem).start()

            @pl.when(me != head)
            def _():
                give_sum(0, head)

            for n in some:

                @pl.when(jnp.logical_and(origin(steps[n]) == 0, me != head))
                def _():
                    give_row(0, head)

            give_sums(0)
        for n in sorted(some, key=lambda n: -steps[n][1]):
            give_rows(steps[n], late)
    give_sums(1)

    some = pl.ds(0, devices - 1)
    pltpu.make_async_copy(send.at[some], send.at[some], send_sem).wait()
    pltpu.make_async_copy(ready.at[some], ready.at[some], gs_out_sem).wait()
    few = pl.ds(0, blocks - 1)
    pltpu.make_async_copy(send_f.at[few], send_f.at[few], send_f_sem).wait()
    pltpu.make_async_copy(out_gf.at[some], out_gf.at[some], gf_out_sem).wait()
    pltpu.make_async_copy(out_gs, out_gs, gs_in_sem).wait()
    pltpu.make_async_copy(out_gf, out_gf, gf_in_sem).wait()


def identity():
    rows = lax.broadcasted_iota(jnp.int32, (LANES, LANES), 0)
    cols = lax.broadcasted_iota(jnp.int32, (LANES, LANES), 1)
    return (rows == cols).astype(f32).astype(bf16)


def place_columns(quarters, gs_in, gf_in, gs_ref, gf_ref):
    eye = identity()
    per = LANES // 2
    for q in range(quarters):
        for source, target in ((gs_in, gs_ref), (gf_in, gf_ref)):
            block = source[pl.ds(q * per, per)].reshape(LANES, LANES)
            target[:, pl.ds(q * LANES, LANES)] = dot_nt(eye, block).astype(bf16)


def body(groups, blocks, signal, cotangent, long_filter):
    positions, columns = signal.shape
    devices = groups * blocks
    tables = make_tables(blocks) + (permutation(LANES // 2).astype(ml_dtypes.bfloat16),)
    vmem = pltpu.VMEM
    dma = pltpu.SemaphoreType.DMA
    anywhere = pl.BlockSpec(memory_space=pl.ANY)
    whole = pl.BlockSpec(memory_space=pltpu.VMEM)
    pairs = pltpu.VMEM((devices, 2, LANES), bf16)
    gs_rows, gf_rows = pl.pallas_call(
        functools.partial(exchange, groups, blocks),
        name="exchange",
        out_shape=(pairs, pairs),
        in_specs=[anywhere] * (3 + len(tables)),
        out_specs=(whole, whole),
        scratch_shapes=[vmem((positions, columns), bf16)] * 3
        + [vmem(table.shape, table.dtype) for table in tables]
        + [
            vmem((devices, 4, LANES), bf16),
            vmem((devices, 2, LANES), bf16),
            vmem((devices, 4, LANES), bf16),
            vmem((blocks, 2, LANES), bf16),
            vmem((devices, 2, LANES), bf16),
            vmem((blocks, 2, LANES), bf16),
            dma((3 + len(tables),)),
            dma(()),
            dma((groups,)),
            dma(()),
            dma(()),
            dma(()),
            dma(()),
            dma(()),
            dma(()),
        ],
        compiler_params=pltpu.CompilerParams(collective_id=0, has_side_effects=True),
    )(signal, cotangent, long_filter, *[jnp.asarray(table) for table in tables])
    gs_rows, gf_rows = (
        pltpu.with_memory_space_constraint(rows, pltpu.VMEM) for rows in (gs_rows, gf_rows)
    )
    result = jax.ShapeDtypeStruct((positions, columns), bf16)
    return pl.pallas_call(
        functools.partial(place_columns, columns // LANES),
        name="place_columns",
        out_shape=(result, result),
        in_specs=[whole] * 2,
        out_specs=(whole, whole),
    )(gs_rows, gf_rows)


def solution(mesh):
    in_specs = (P("cp", "tp"), P("cp", "tp"), P("cp", None))
    out_specs = (P("cp", "tp"), P("cp", None))
    run = functools.partial(body, mesh.shape["tp"], mesh.shape["cp"])
    return jax.shard_map(run, mesh=mesh, in_specs=in_specs, out_specs=out_specs, check_vma=False)
```
